256 devices in a mesh: row: 32 (over y, x, z_hi), col: 8 (over z_lo, core).
Axes of the slice: x: 4, y: 4, z: 8 (z_hi: 2, z_lo: 4; z = z_hi * 4 + z_lo), core: 2. Of those that a mesh axis runs over, the one named last changes fastest.
Arguments:
- density: bfloat16 [6144, 5, 64, 64], P(('row', 'col')), may hold values from -0.29882812 to 0.29882812
- margin: bfloat16 [6144, 5, 64, 64], P(('row', 'col')), may hold values from -6 to 6
- potential: float32 [32, 32, 2048], P('row', None, 'col'), may hold values from -6 to 6
- basis_values: bfloat16 [2048, 8, 64, 1024], P(('row', 'col')), may hold values from -1.1953125 to 1.1953125
- pair_owner: int32 [6144, 5, 1], P(('row', 'col')), may hold values from 0 to 255; in each aligned block of 120 rows (0 to 119, 120 to 239, ..., all dimensions but the last counted through in order) at most 2 rows name the same one
- pair_box: int32 [6144, 5], P(('row', 'col')), may hold values from 0 to 7
- pair_slots: int32 [6144, 5, 2], P(('row', 'col')), may hold values from 0 to 7
Outputs:
- density_grid: float32 [32, 32, 2048], P(None, 'row', 'col')
- ks_blocks: bfloat16 [6144, 5, 64, 64], P(('row', 'col'))
- margin_product: bfloat16 [6144, 5, 64, 64], P(('row', 'col'))
The draws below stay inside these ranges and needn't reach their ends.
Inputs may be any that keep to these rules, and one draw needn't show every extreme that they name: `pair_owner`: among the pairs of one device's atoms, at most 2 name the same owner, and exactly 2 do for some owner.
All inputs are finite; a program needn't handle non-finite values.
Results may differ from the reference program's by a relative error of at most 0.0049.
Values may be sent and summed in bfloat16 or wider, within the bound.
A program may use at most 128 MiB of HBM per device.

```python
import math
import jax
import jax.numpy as jnp
import numpy as np
from jax import lax

BF = 64
HALF = 2
SLOTS = 8
ZS = 256
BX = 4
NOFF = 5
NATOM = 6144
PAIRS_DEV = 120
CAP = 2
GX = 32
GY = 32
GZ = 2048
TPD = 8
BOXP = 1024
NTASK = 2048
N_ROW = 32
N_COL = 8
DEVICES = 256


def with_ends(entries, rng, low, high):
    shape = entries.shape
    spot = [jax.random.randint(jax.random.fold_in(rng, axis), (), 0, shape[axis]) for axis in range(len(shape))]
    entries = entries.at[tuple(spot)].set(low)
    longest = shape.index(max(shape))
    spot[longest] = (spot[longest] + 1) % shape[longest]
    return entries.at[tuple(spot)].set(high)


def steps_of(rng, shape, pieces, smallest, high):
    def one(dim, shards_of):
        steps = jax.random.uniform(jax.random.fold_in(jax.random.fold_in(rng, 6), dim), (shards_of,), jnp.float32, smallest / len(pieces), high / len(pieces))
        return jnp.repeat(jnp.exp(steps), shape[dim] // shards_of).reshape((-1,) + (1,) * (len(shape) - dim - 1))

    factor_of = one(*pieces[0])
    for cut in pieces[1:]:
        factor_of = factor_of * one(*cut)
    return factor_of


def deal_out(own_key, own, number, rows, amount, top, limit, skew):
    order = jax.random.permutation(own_key, amount)
    crowded, common = load_shares(amount, rows * top, limit, skew, True), load_shares(amount, rows * top, limit, skew, False)
    places = jnp.arange(amount)

    def named(lengths, turn):
        used = int((lengths > 0).sum())
        fixed = max(1, used // 4)
        moved = fixed + (places - fixed + turn * (used - fixed)) % max(1, amount - fixed)
        return jnp.zeros((amount,), jnp.int32).at[order[jnp.where(places < fixed, places, moved)]].set(jnp.asarray(lengths, jnp.int32))

    lengths = jnp.where(number % 4 == 0, named(crowded, number // 4), named(common, number - number // 4 - 1))
    mixed = jax.random.permutation(jax.random.fold_in(own, 3), amount)
    source_of, sink = mixed[0:amount // 2 * 2:2], mixed[1:amount // 2 * 2:2]
    room = jnp.minimum(lengths[source_of] - 1, limit - lengths[sink]) // 2
    room = jnp.where((source_of == order[0]) | (sink == order[0]) | (lengths[sink] == 0), 0, jnp.maximum(room, 0))
    moved = jax.random.randint(jax.random.fold_in(own, 4), (amount // 2,), 0, 1 << 20) % (room + 1)
    lengths = lengths.at[source_of].add(-moved).at[sink].add(moved)
    items = jnp.searchsorted(jnp.cumsum(lengths), jnp.arange(rows * top), side="right").astype(jnp.int32)
    listing = items.reshape(top, rows).T
    listing = listing[jax.random.permutation(jax.random.fold_in(own, 1), rows)]
    turn = jax.random.randint(jax.random.fold_in(own, 2), (rows, 1), 0, top)
    return jnp.take_along_axis(listing, (jnp.arange(top)[None, :] + turn) % top, axis=1)


def load_shares(number_of, total, bound, skew, full):
    weights = [(1 << 20) // math.isqrt(standing ** skew) + 1 for standing in range(1, number_of + 1)]
    largest = bound if full else min(bound, max(-(-total // number_of), total * weights[0] // sum(weights)))
    least = 1 if total - largest >= number_of - 1 else 0
    given, spare = [largest] + [least] * (number_of - 1), total - largest - least * (number_of - 1)
    while spare > 0:
        free = [i for i in range(1, number_of) if given[i] < largest] or [i for i in range(1, number_of) if given[i] < bound]
        mass, budget = sum([weights[i] for i in free]), spare
        for i in free:
            extra = min(bound - given[i], max(1, budget * weights[i] // mass), spare)
            given[i] = given[i] + extra
            spare = spare - extra
    return np.array(given)


def normal_values(stream_key, shape, scale, limit, pieces=(), kind=jnp.bfloat16):
    values = scale * jax.random.normal(stream_key, shape, jnp.float32)
    if pieces:
        values = values * steps_of(stream_key, shape, pieces, -0.22, 0.18)
    return jnp.clip(values, -limit, limit).astype(kind)


def setup_inputs(seed: int = 0) -> dict:
    streams_of = jax.random.split(jax.random.key(seed), 8)
    density = normal_values(streams_of[0], (NATOM, NOFF, BF, BF), 0.05, 0.29882812, ((0, 256),))
    margin = normal_values(streams_of[1], (NATOM, NOFF, BF, BF), 1.0, 6.0, ((0, 256),))
    potential = normal_values(streams_of[2], (GX, GY, GZ), 1.0, 6.0, ((0, 32), (2, 8)), jnp.float32)
    basis_values = normal_values(streams_of[3], (NTASK, SLOTS, BF, BOXP), 0.2, 1.1953125, ((0, 256),))
    pair_owner_keys = jax.random.split(jax.random.fold_in(streams_of[4], 1), NATOM * NOFF // PAIRS_DEV)
    pair_owner_turns = jax.random.permutation(jax.random.fold_in(streams_of[4], 3), NATOM * NOFF // PAIRS_DEV)
    pair_owner = jax.vmap(lambda own, number: deal_out(jax.random.fold_in(streams_of[4], 2), own, number, PAIRS_DEV, DEVICES, 1, CAP, 2))(pair_owner_keys, pair_owner_turns).reshape((NATOM, NOFF, 1))
    pair_box = with_ends(jax.random.randint(streams_of[5], (NATOM, NOFF), 0, TPD), jax.random.fold_in(streams_of[5], 1), 0, TPD - 1).astype(jnp.int32)
    pair_slots = with_ends(jax.random.randint(streams_of[6], (NATOM, NOFF, 2), 0, SLOTS), jax.random.fold_in(streams_of[6], 1), 0, SLOTS - 1).astype(jnp.int32)
    return {"density": density, "margin": margin, "potential": potential, "basis_values": basis_values, "pair_owner": pair_owner, "pair_box": pair_box, "pair_slots": pair_slots}


def reference(density, margin, potential, basis_values, pair_owner, pair_box, pair_slots):
    pair_total = NATOM * NOFF
    tasks = (pair_owner.reshape(pair_total) * TPD + pair_box.reshape(pair_total)).astype(jnp.int32)
    firsts = pair_slots[..., 0].reshape(pair_total).astype(jnp.int32)
    seconds = pair_slots[..., 1].reshape(pair_total).astype(jnp.int32)
    task_potential = potential.reshape(TPD, BX, N_ROW, N_COL, ZS).transpose(2, 3, 0, 1, 4).reshape(NTASK, BOXP)
    blocks = density.reshape(pair_total, BF, BF)
    group = PAIRS_DEV * 4
    groups = pair_total // group
    highest = lax.Precision.HIGHEST

    def step(grid, packet):
        block_part, task_part, first_part, second_part = packet
        first_basis = basis_values[task_part, first_part].astype(jnp.float32)
        second_basis = basis_values[task_part, second_part].astype(jnp.float32)
        weighted = jnp.einsum("sij,sjg->sig", block_part.astype(jnp.float32), second_basis, precision=highest)
        contrib = jnp.sum(first_basis * weighted, axis=1)
        scaled = (first_basis * task_potential[task_part][:, None, :]).astype(jnp.bfloat16)
        scaled = lax.optimization_barrier(scaled)
        matrix = jnp.einsum("sig,sjg->sij", scaled.astype(jnp.float32), second_basis, precision=highest)
        return grid.at[task_part].add(contrib), matrix.astype(jnp.bfloat16)

    packets = (blocks.reshape(groups, group, BF, BF), tasks.reshape(groups, group),
               firsts.reshape(groups, group), seconds.reshape(groups, group))
    grid, matrices = lax.scan(step, jnp.zeros((NTASK, BOXP), jnp.float32), packets)
    density_grid = grid.reshape(N_ROW, N_COL, TPD, BX, ZS).transpose(2, 3, 0, 1, 4).reshape(GX, GY, GZ)
    ks_blocks = matrices.reshape(NATOM, NOFF, BF, BF)
    columns = []
    for offset in range(NOFF):
        total = jnp.zeros((NATOM, BF, BF), jnp.float32)
        for middle in range(NOFF):
            inner = offset - middle + HALF
            if 0 <= inner < NOFF:
                moved = jnp.roll(margin[:, inner], -(middle - HALF), axis=0)
                total = total + jnp.einsum("aik,akj->aij", density[:, middle].astype(jnp.float32),
                                           moved.astype(jnp.float32), precision=highest)
        columns.append(total)
    margin_product = jnp.stack(columns, axis=1).astype(jnp.bfloat16)
    return density_grid, ks_blocks, margin_product
```

```python
import functools

import jax
import jax.numpy as jnp
from jax import lax
from jax.experimental import pallas as pl
from jax.experimental.pallas import tpu as pltpu
from jax.sharding import PartitionSpec as P

HALF = 2
PAIRS = 120
PEERS = 256
SLOTS_ALL = 512
ROWS = 32
LANES = 128
BF = 64
TASKS = 8
BASIS = 512
POINTS = 1024
ALL = ("row", "col")
VMEM_LIMIT = 56 * 1024 * 1024


def padded(array, sides, width):
    for axis, dim in sides:
        size, length = (lax.axis_size(axis), array.shape[dim])
        up = [(i, (i + 1) % size) for i in range(size)]
        down = [(j, i) for i, j in up]
        last = lax.slice_in_dim(array, length - width, length, axis=dim)
        first = lax.slice_in_dim(array, 0, width, axis=dim)
        before = lax.ppermute(last, axis, up)
        after = lax.ppermute(first, axis, down)
        array = jnp.concatenate([before, array, after], axis=dim)
    return array


def margin_of(density, margin):
    atoms_here = density.shape[0]
    offsets = density.shape[1]
    extended = padded(margin, ((ALL, 0),), HALF)
    columns = []
    for offset in range(offsets):
        lowest = max(0, offset - HALF)
        highest = min(offsets - 1, offset + HALF)
        left_blocks = density[:, lowest : highest + 1]
        right_blocks = jnp.stack(
            [extended[middle : middle + atoms_here, offset - middle + HALF] for middle in range(lowest, highest + 1)],
            axis=1,
        )
        columns.append(jnp.einsum("amik,amkj->aij", left_blocks, right_blocks, preferred_element_type=jnp.float32))
    return jnp.stack(columns, axis=1).astype(jnp.bfloat16)


def pack_kernel(place, density, out):
    def body(step, carry):
        for inner in range(8):
            pair = step * 8 + inner
            block = density[pair]
            spot = place[pair]
            out[spot, :, 0:BF] = block[0:ROWS]
            out[spot, :, BF:LANES] = block[ROWS:BF]
        return carry

    lax.fori_loop(0, PAIRS // 8, body, 0)


def unpack_kernel(place, blocks, out):
    def body(step, carry):
        for inner in range(8):
            pair = step * 8 + inner
            block = blocks[place[pair]]
            out[pair, 0:ROWS] = block[:, 0:BF]
            out[pair, ROWS:BF] = block[:, BF:LANES]
        return carry

    lax.fori_loop(0, PAIRS // 8, body, 0)


def matrix_kernel(label, basis, potential, out, scaled, table):
    task = pl.program_id(0)
    phi = basis[0]
    scaled[...] = (phi.astype(jnp.float32) * potential[0]).astype(jnp.bfloat16)
    full = lax.dot_general(
        scaled[...], phi, (((1,), (1,)), ((), ())), preferred_element_type=jnp.float32
    )
    left = lax.broadcasted_iota(jnp.int32, (ROWS, LANES), 1) < BF
    for first in range(8):
        for pair in range(4):
            columns = slice(pair * LANES, (pair + 1) * LANES)
            top = full[first * BF : first * BF + ROWS, columns]
            low = full[first * BF + ROWS : (first + 1) * BF, columns]
            spot = task * 64 + first * 8 + 2 * pair
            table[spot] = jnp.where(left, top, pltpu.roll(low, BF, 1)).astype(jnp.bfloat16)
            table[spot + 1] = jnp.where(left, pltpu.roll(top, BF, 1), low).astype(jnp.bfloat16)

    @pl.when(task == TASKS - 1)
    def _():
        def body(step, carry):
            for inner in range(16):
                slot = step * 16 + inner
                out[slot] = table[jnp.maximum(label[slot], 0)]
            return carry

        lax.fori_loop(0, SLOTS_ALL // 16, body, 0)


def grid_kernel(label, blocks, basis, out, table, weights):
    task = pl.program_id(0)

    @pl.when(task == 0)
    def _():
        def clear(step, carry):
            for inner in range(8):
                table[step * 8 + inner] = jnp.zeros((ROWS, LANES), jnp.float32)
            return carry

        lax.fori_loop(0, SLOTS_ALL // 8, clear, 0)

        def body(step, carry):
            for inner in range(8):
                slot = step * 8 + inner
                which = label[slot]
                spot = jnp.where(which < 0, SLOTS_ALL, which)
                table[spot] = table[spot] + blocks[slot].astype(jnp.float32)
            return carry

        lax.fori_loop(0, SLOTS_ALL // 8, body, 0)

    left = lax.broadcasted_iota(jnp.int32, (ROWS, LANES), 1) < BF
    for first in range(8):
        for pair in range(4):
            spot = task * 64 + first * 8 + 2 * pair
            one = table[spot]
            two = table[spot + 1]
            columns = slice(pair * LANES, (pair + 1) * LANES)
            weights[first * BF : first * BF + ROWS, columns] = jnp.where(left, one, pltpu.roll(two, BF, 1)).astype(
                jnp.bfloat16
            )
            weights[first * BF + ROWS : (first + 1) * BF, columns] = jnp.where(left, pltpu.roll(one, BF, 1), two).astype(
                jnp.bfloat16
            )
    for piece in range(4):
        columns = slice(piece * 256, (piece + 1) * 256)
        phi = basis[0, :, columns]
        weighted = jnp.dot(weights[...], phi, preferred_element_type=jnp.float32)
        out[0, :, columns] = jnp.sum(phi.astype(jnp.float32) * weighted, axis=0, keepdims=True)


def params(**more):
    return pltpu.CompilerParams(vmem_limit_bytes=VMEM_LIMIT, **more)


SMEM = pl.BlockSpec(memory_space=pltpu.SMEM)
BLOCKS = jax.ShapeDtypeStruct((SLOTS_ALL, ROWS, LANES), jnp.bfloat16)


def whole(shape):
    return pl.BlockSpec(shape, lambda *_: (0,) * len(shape))


def local(density, margin, potential, basis_values, pair_owner, pair_box, pair_slots):
    atoms_here, offsets = density.shape[:2]
    owners = pair_owner.reshape(PAIRS)
    same = owners[:, None] == owners[None, :]
    before = jnp.arange(PAIRS)[:, None] > jnp.arange(PAIRS)[None, :]
    ranks = jnp.sum((same & before).astype(jnp.int32), axis=1)
    places = owners * 2 + ranks
    fields = jnp.stack(
        [pair_box.reshape(PAIRS), pair_slots[..., 0].reshape(PAIRS), pair_slots[..., 1].reshape(PAIRS)], axis=0
    )
    chosen = jnp.arange(SLOTS_ALL, dtype=jnp.int32)[None, :, None] == places[None, None, :]
    sent = jnp.sum(jnp.where(chosen, fields[:, None, :] + 1, 0), axis=2) - 1
    sent = sent.reshape(3, PEERS, 2).transpose(1, 0, 2).reshape(PEERS, 1, 6)
    sent = jnp.pad(sent, ((0, 0), (0, 0), (0, LANES - 6)))
    tags = lax.all_to_all(sent, ALL, 0, 0, tiled=True).reshape(PEERS, LANES)[:, :6].reshape(PEERS, 3, 2)
    labels = jnp.where(tags[:, 0] < 0, -1, tags[:, 0] * 64 + tags[:, 1] * 8 + tags[:, 2]).reshape(SLOTS_ALL)

    flat = density.reshape(PAIRS, BF, BF)
    outgoing = pl.pallas_call(
        pack_kernel,
        out_shape=BLOCKS,
        in_specs=[SMEM, pl.BlockSpec(memory_space=pltpu.VMEM)],
        out_specs=pl.BlockSpec(memory_space=pltpu.VMEM),
        compiler_params=params(),
        cost_estimate=pl.CostEstimate(flops=0, bytes_accessed=6 << 20, transcendentals=0),
        name="pack",
    )(places, flat)
    arrived = lax.all_to_all(outgoing.reshape(PEERS, 64, LANES), ALL, 0, 0, tiled=True).reshape(BLOCKS.shape)

    pencil = lax.all_to_all(potential, "row", split_axis=1, concat_axis=0, tiled=True)
    box_potential = pencil.reshape(TASKS, 1, POINTS)
    phi = basis_values.reshape(TASKS, BASIS, POINTS)

    results = pl.pallas_call(
        matrix_kernel,
        out_shape=BLOCKS,
        grid=(TASKS,),
        in_specs=[
            SMEM,
            pl.BlockSpec((1, BASIS, POINTS), lambda t: (t, 0, 0)),
            pl.BlockSpec((1, 1, POINTS), lambda t: (t, 0, 0)),
        ],
        out_specs=whole(BLOCKS.shape),
        scratch_shapes=[
            pltpu.VMEM((BASIS, POINTS), jnp.bfloat16),
            pltpu.VMEM((SLOTS_ALL, ROWS, LANES), jnp.bfloat16),
        ],
        compiler_params=params(),
        cost_estimate=pl.CostEstimate(flops=2 * TASKS * BASIS * BASIS * POINTS, bytes_accessed=14 << 20, transcendentals=0),
        name="matrices",
    )(labels, phi, box_potential)
    returned = lax.all_to_all(results.reshape(PEERS, 64, LANES), ALL, 0, 0, tiled=True).reshape(BLOCKS.shape)

    grid_rows = pl.pallas_call(
        grid_kernel,
        out_shape=jax.ShapeDtypeStruct((TASKS, 1, POINTS), jnp.float32),
        grid=(TASKS,),
        in_specs=[SMEM, whole(BLOCKS.shape), pl.BlockSpec((1, BASIS, POINTS), lambda t: (t, 0, 0))],
        out_specs=pl.BlockSpec((1, 1, POINTS), lambda t: (t, 0, 0)),
        scratch_shapes=[
            pltpu.VMEM((SLOTS_ALL + 1, ROWS, LANES), jnp.float32),
            pltpu.VMEM((BASIS, BASIS), jnp.bfloat16),
        ],
        compiler_params=params(),
        cost_estimate=pl.CostEstimate(flops=2 * TASKS * BASIS * BASIS * POINTS, bytes_accessed=14 << 20, transcendentals=0),
        name="collocate",
    )(labels, arrived, phi)
    density_grid = grid_rows.reshape(pencil.shape)

    ks_blocks = pl.pallas_call(
        unpack_kernel,
        out_shape=jax.ShapeDtypeStruct((PAIRS, BF, BF), jnp.bfloat16),
        in_specs=[SMEM, pl.BlockSpec(memory_space=pltpu.VMEM)],
        out_specs=pl.BlockSpec(memory_space=pltpu.VMEM),
        compiler_params=params(),
        cost_estimate=pl.CostEstimate(flops=0, bytes_accessed=6 << 20, transcendentals=0),
        name="unpack",
    )(places, returned).reshape(atoms_here, offsets, BF, BF)
    return density_grid, ks_blocks, margin_of(density, margin)


def solution(mesh):
    placed = (
        P(ALL, None, None, None),
        P(ALL, None, None, None),
        P("row", None, "col"),
        P(ALL, None, None, None),
        P(ALL, None, None),
        P(ALL, None),
        P(ALL, None, None),
    )
    return jax.shard_map(
        local,
        mesh=mesh,
        in_specs=placed,
        out_specs=(P(None, "row", "col"), P(ALL, None, None, None), P(ALL, None, None, None)),
        check_vma=False,
    )
```

```python
import functools

import jax
import jax.numpy as jnp
from jax import lax
from jax.experimental import pallas as pl
from jax.experimental.pallas import tpu as pltpu
from jax.sharding import PartitionSpec as P

HALF = 2
PAIRS = 120
PEERS = 256
SLOTS_ALL = 512
ROWS = 32
LANES = 128
BF = 64
TASKS = 8
BASIS = 512
POINTS = 1024
ALL = ("row", "col")
ZS = 8
PLANE = 32
CAP = 32
HELD = ZS * CAP
MESH = pl.DeviceIdType.MESH
VMEM_LIMIT = 56 * 1024 * 1024


def padded(array, sides, width):
    for axis, dim in sides:
        size, length = (lax.axis_size(axis), array.shape[dim])
        up = [(i, (i + 1) % size) for i in range(size)]
        down = [(j, i) for i, j in up]
        last = lax.slice_in_dim(array, length - width, length, axis=dim)
        first = lax.slice_in_dim(array, 0, width, axis=dim)
        before = lax.ppermute(last, axis, up)
        after = lax.ppermute(first, axis, down)
        array = jnp.concatenate([before, array, after], axis=dim)
    return array


def margin_of(density, margin):
    atoms_here = density.shape[0]
    offsets = density.shape[1]
    extended = padded(margin, ((ALL, 0),), HALF)
    columns = []
    for offset in range(offsets):
        lowest = max(0, offset - HALF)
        highest = min(offsets - 1, offset + HALF)
        left_blocks = density[:, lowest : highest + 1]
        right_blocks = jnp.stack(
            [extended[middle : middle + atoms_here, offset - middle + HALF] for middle in range(lowest, highest + 1)],
            axis=1,
        )
        columns.append(jnp.einsum("amik,amkj->aij", left_blocks, right_blocks, preferred_element_type=jnp.float32))
    return jnp.stack(columns, axis=1).astype(jnp.bfloat16)


def pack_kernel(place, density, out):
    def body(step, carry):
        for inner in range(8):
            pair = step * 8 + inner
            block = density[pair]
            spot = place[pair]
            out[spot, :, 0:BF] = block[0:ROWS]
            out[spot, :, BF:LANES] = block[ROWS:BF]
        return carry

    lax.fori_loop(0, PAIRS // 8, body, 0)


def unpack_kernel(place, blocks, out):
    def body(step, carry):
        for inner in range(8):
            pair = step * 8 + inner
            block = blocks[place[pair]]
            out[pair, 0:ROWS] = block[:, 0:BF]
            out[pair, ROWS:BF] = block[:, BF:LANES]
        return carry

    lax.fori_loop(0, PAIRS // 8, body, 0)


def exchange_kernel(zsend, psend, zrecv, precv, zs, zr, ps, pr, own):
    row, col = lax.axis_index("row"), lax.axis_index("col")
    y, x, high = row // 8, lax.rem(row // 2, 4), lax.rem(row, 2)
    low, core = col // 2, lax.rem(col, 2)
    z = high * 4 + low
    here = (y * 4 + x) * 2 + core

    def along(step):
        to = lax.rem(z + step, ZS)
        return to, (y * 8 + x * 2 + to // 4, lax.rem(to, 4) * 2 + core)

    def across(dy, dx, dc):
        to_y, to_x, to_c = lax.rem(y + dy, 4), lax.rem(x + dx, 4), lax.rem(core + dc, 2)
        return (to_y * 4 + to_x) * 2 + to_c, (to_y * 8 + to_x * 2 + high, low * 2 + to_c)

    zsteps = (4, 3, 5, 2, 6, 1, 7)
    psteps = [
        (dy, dx, dc)
        for dy, dx in (
            (2, 2), (1, 3), (3, 1), (1, 1), (3, 3), (2, 1), (2, 3), (1, 2), (3, 2), (0, 2), (2, 0), (0, 1), (0, 3), (1, 0), (3, 0), (0, 0),
        )
        for dc in (0, 1)
        if (dy, dx, dc) != (0, 0, 0)
    ]
    barrier = pltpu.get_barrier_semaphore()
    for step in zsteps:
        pl.semaphore_signal(barrier, inc=1, device_id=along(step)[1], device_id_type=MESH)
    for steps in psteps:
        pl.semaphore_signal(barrier, inc=1, device_id=across(*steps)[1], device_id_type=MESH)
    pl.semaphore_wait(barrier, len(zsteps) + len(psteps))
    copies = []
    for number in range(len(psteps)):
        if number < len(zsteps):
            to, where = along(zsteps[number])
            copies.append(
                pltpu.make_async_remote_copy(
                    src_ref=zsend.at[to], dst_ref=zrecv.at[z], send_sem=zs.at[number], recv_sem=zr.at[number],
                    device_id=where, device_id_type=MESH,
                )
            )
            copies[-1].start()
        to, where = across(*psteps[number])
        copies.append(
            pltpu.make_async_remote_copy(
                src_ref=psend.at[to], dst_ref=precv.at[here], send_sem=ps.at[number], recv_sem=pr.at[number],
                device_id=where, device_id_type=MESH,
            )
        )
        copies[-1].start()
    mine = [
        pltpu.make_async_copy(zsend.at[z], zrecv.at[z], own.at[0]),
        pltpu.make_async_copy(psend.at[here], precv.at[here], own.at[1]),
    ]
    for copy in mine:
        copy.start()
    for copy in mine + copies:
        copy.wait()


def exchange(zsend, psend, number):
    hbm = pl.BlockSpec(memory_space=pl.ANY)
    return pl.pallas_call(
        exchange_kernel,
        out_shape=(
            jax.ShapeDtypeStruct((ZS, CAP * ROWS, LANES), jnp.bfloat16),
            jax.ShapeDtypeStruct((PLANE, 16 * ROWS, LANES), jnp.bfloat16),
        ),
        in_specs=[hbm, hbm],
        out_specs=(hbm, hbm),
        scratch_shapes=[
            pltpu.SemaphoreType.DMA((7,)),
            pltpu.SemaphoreType.DMA((7,)),
            pltpu.SemaphoreType.DMA((31,)),
            pltpu.SemaphoreType.DMA((31,)),
            pltpu.SemaphoreType.DMA((2,)),
        ],
        compiler_params=params(collective_id=number, has_side_effects=True),
        name="exchange",
    )(zsend, psend)


def swap_kernel(spot, held, results, out, back):
    def body(step, carry):
        for inner in range(8):
            item = step * 8 + inner
            where = spot[item]
            out[where] = held[item]
            back[item] = results[jnp.minimum(where, SLOTS_ALL - 1)]
        return carry

    lax.fori_loop(0, HELD // 8, body, 0)


def matrix_kernel(label, basis, potential, out, scaled, table):
    task = pl.program_id(0)
    phi = basis[0]
    scaled[...] = (phi.astype(jnp.float32) * potential[0]).astype(jnp.bfloat16)
    full = lax.dot_general(
        scaled[...], phi, (((1,), (1,)), ((), ())), preferred_element_type=jnp.float32
    )
    left = lax.broadcasted_iota(jnp.int32, (ROWS, LANES), 1) < BF
    for first in range(8):
        for pair in range(4):
            columns = slice(pair * LANES, (pair + 1) * LANES)
            top = full[first * BF : first * BF + ROWS, columns]
            low = full[first * BF + ROWS : (first + 1) * BF, columns]
            spot = task * 64 + first * 8 + 2 * pair
            table[spot] = jnp.where(left, top, pltpu.roll(low, BF, 1)).astype(jnp.bfloat16)
            table[spot + 1] = jnp.where(left, pltpu.roll(top, BF, 1), low).astype(jnp.bfloat16)

    @pl.when(task == TASKS - 1)
    def _():
        def body(step, carry):
            for inner in range(16):
                slot = step * 16 + inner
                out[slot] = table[jnp.maximum(label[slot], 0)]
            return carry

        lax.fori_loop(0, SLOTS_ALL // 16, body, 0)


def grid_kernel(label, blocks, basis, out, table, weights):
    task = pl.program_id(0)

    @pl.when(task == 0)
    def _():
        def clear(step, carry):
            for inner in range(8):
                table[step * 8 + inner] = jnp.zeros((ROWS, LANES), jnp.float32)
            return carry

        lax.fori_loop(0, SLOTS_ALL // 8, clear, 0)

        def body(step, carry):
            for inner in range(8):
                slot = step * 8 + inner
                which = label[slot]
                spot = jnp.where(which < 0, SLOTS_ALL, which)
                table[spot] = table[spot] + blocks[slot].astype(jnp.float32)
            return carry

        lax.fori_loop(0, SLOTS_ALL // 8, body, 0)

    left = lax.broadcasted_iota(jnp.int32, (ROWS, LANES), 1) < BF
    for first in range(8):
        for pair in range(4):
            spot = task * 64 + first * 8 + 2 * pair
            one = table[spot]
            two = table[spot + 1]
            columns = slice(pair * LANES, (pair + 1) * LANES)
            weights[first * BF : first * BF + ROWS, columns] = jnp.where(left, one, pltpu.roll(two, BF, 1)).astype(
                jnp.bfloat16
            )
            weights[first * BF + ROWS : (first + 1) * BF, columns] = jnp.where(left, pltpu.roll(one, BF, 1), two).astype(
                jnp.bfloat16
            )
    for piece in range(4):
        columns = slice(piece * 256, (piece + 1) * 256)
        phi = basis[0, :, columns]
        weighted = jnp.dot(weights[...], phi, preferred_element_type=jnp.float32)
        out[0, :, columns] = jnp.sum(phi.astype(jnp.float32) * weighted, axis=0, keepdims=True)


def params(**more):
    return pltpu.CompilerParams(vmem_limit_bytes=VMEM_LIMIT, **more)


SMEM = pl.BlockSpec(memory_space=pltpu.SMEM)
VM = pl.BlockSpec(memory_space=pltpu.VMEM)
BLOCKS = jax.ShapeDtypeStruct((SLOTS_ALL, ROWS, LANES), jnp.bfloat16)


def whole(shape):
    return pl.BlockSpec(shape, lambda *_: (0,) * len(shape))


def packed(places, flat, blocks):
    return pl.pallas_call(
        pack_kernel,
        out_shape=jax.ShapeDtypeStruct((blocks, ROWS, LANES), jnp.bfloat16),
        in_specs=[SMEM, VM],
        out_specs=VM,
        compiler_params=params(),
        cost_estimate=pl.CostEstimate(flops=0, bytes_accessed=6 << 20, transcendentals=0),
        name="pack",
    )(places, flat)


def unpacked(places, blocks):
    return pl.pallas_call(
        unpack_kernel,
        out_shape=jax.ShapeDtypeStruct((PAIRS, BF, BF), jnp.bfloat16),
        in_specs=[SMEM, VM],
        out_specs=VM,
        compiler_params=params(),
        cost_estimate=pl.CostEstimate(flops=0, bytes_accessed=6 << 20, transcendentals=0),
        name="unpack",
    )(places, blocks)


def swapped(spot, held, results):
    return pl.pallas_call(
        swap_kernel,
        out_shape=(
            jax.ShapeDtypeStruct((SLOTS_ALL + 16, ROWS, LANES), jnp.bfloat16),
            jax.ShapeDtypeStruct((HELD, ROWS, LANES), jnp.bfloat16),
        ),
        in_specs=[SMEM, VM, VM],
        out_specs=(VM, VM),
        compiler_params=params(),
        name="swap",
    )(spot, held, results)


def by_plane(values):
    rest = values.shape[1:]
    return values.reshape((16, 8, 2) + rest).swapaxes(1, 2).reshape((PEERS,) + rest)


def by_mesh(values):
    rest = values.shape[1:]
    return values.reshape((16, 2, 8) + rest).swapaxes(1, 2).reshape((PEERS,) + rest)


def local(density, margin, potential, basis_values, pair_owner, pair_box, pair_slots):
    atoms_here, offsets = density.shape[:2]
    row, col = lax.axis_index("row"), lax.axis_index("col")
    owners = pair_owner.reshape(PAIRS)
    planes = (owners // 8) % 2 * 4 + owners % 8 // 2
    inside = owners // 16 * 2 + owners % 2
    before = jnp.arange(PAIRS)[:, None] > jnp.arange(PAIRS)[None, :]
    ranks = jnp.sum(((owners[:, None] == owners[None, :]) & before).astype(jnp.int32), axis=1)
    turns = jnp.sum(((planes[:, None] == planes[None, :]) & before).astype(jnp.int32), axis=1)
    places = owners * 2 + ranks
    spots = jnp.where(turns < CAP, planes * CAP + turns, HELD)
    flat = density.reshape(PAIRS, BF, BF)
    held = packed(spots, flat, HELD + CAP)

    fields = jnp.stack(
        [pair_box.reshape(PAIRS), pair_slots[..., 0].reshape(PAIRS), pair_slots[..., 1].reshape(PAIRS)], axis=0
    )
    chosen = jnp.arange(SLOTS_ALL, dtype=jnp.int32)[None, :, None] == places[None, None, :]
    tags = jnp.sum(jnp.where(chosen, fields[:, None, :] + 1, 0), axis=2) - 1
    tags = tags.reshape(3, PEERS, 2).transpose(1, 0, 2).reshape(PEERS, 6)
    listed = jnp.arange(HELD, dtype=jnp.int32)[:, None] == spots[None, :]
    targets = jnp.sum(jnp.where(listed, (inside * 2 + ranks)[None, :] + 1, 0), axis=1) - 1
    targets = jnp.broadcast_to(targets.reshape(1, ZS, 1, CAP), (16, ZS, 2, CAP)).reshape(PEERS, CAP)
    over = jnp.max(turns) >= CAP
    rows = jnp.broadcast_to(potential[0][:, None, :], (32, 8, 256)).reshape(PEERS, 256)
    notes = jnp.concatenate(
        [tags, jnp.broadcast_to(over.astype(jnp.int32), (PEERS, 2)), targets, jnp.zeros((PEERS, LANES - 8 - CAP), jnp.int32)],
        axis=1,
    ).astype(jnp.float32)
    sent = jnp.concatenate([notes, rows], axis=1).reshape(PEERS, 1, LANES + 256)
    got = lax.all_to_all(sent, ALL, 0, 0, tiled=True).reshape(PEERS, LANES + 256)
    notes = got[:, :LANES].astype(jnp.int32)
    pencil = lax.dynamic_index_in_dim(got[:, LANES:].reshape(32, 8, 256), col, 1, keepdims=False)
    box_potential = pencil.reshape(TASKS, 1, POINTS)
    over = jnp.max(notes[:, 6]) > 0
    tags = by_plane(notes[:, :6]).reshape(PEERS, 3, 2)
    labels = jnp.where(tags[:, 0] < 0, -1, tags[:, 0] * 64 + tags[:, 1] * 8 + tags[:, 2]).reshape(SLOTS_ALL)
    here = row // 2 * 2 + col % 2
    targets = lax.dynamic_index_in_dim(by_plane(notes[:, 8 : 8 + CAP]).reshape(PLANE, ZS, CAP), here, 0, keepdims=False)
    number = jnp.arange(HELD, dtype=jnp.int32).reshape(ZS, CAP)
    routes = jnp.where(targets < 0, SLOTS_ALL + number % 16, targets // 2 * 16 + number // CAP * 2 + targets % 2).reshape(HELD)

    phi = basis_values.reshape(TASKS, BASIS, POINTS)
    results = pl.pallas_call(
        matrix_kernel,
        out_shape=BLOCKS,
        grid=(TASKS,),
        in_specs=[
            SMEM,
            pl.BlockSpec((1, BASIS, POINTS), lambda t: (t, 0, 0)),
            pl.BlockSpec((1, 1, POINTS), lambda t: (t, 0, 0)),
        ],
        out_specs=whole(BLOCKS.shape),
        scratch_shapes=[
            pltpu.VMEM((BASIS, POINTS), jnp.bfloat16),
            pltpu.VMEM((SLOTS_ALL, ROWS, LANES), jnp.bfloat16),
        ],
        compiler_params=params(),
        cost_estimate=pl.CostEstimate(flops=2 * TASKS * BASIS * BASIS * POINTS, bytes_accessed=14 << 20, transcendentals=0),
        name="matrices",
    )(labels, phi, box_potential)

    margin_product = margin_of(density, margin)
    results, margin_product = lax.optimization_barrier((results, margin_product))

    def fast(results, held, flat, places, spots, routes):
        got_z, got_p = exchange(held.reshape(ZS + 1, CAP * ROWS, LANES), results.reshape(PLANE, 16 * ROWS, LANES), 0)
        out, back = swapped(routes, got_z.reshape(HELD, ROWS, LANES), got_p.reshape(BLOCKS.shape))
        back, arrived = exchange(back.reshape(ZS, CAP * ROWS, LANES), out.reshape(PLANE + 1, 16 * ROWS, LANES), 1)
        return arrived.reshape(BLOCKS.shape), unpacked(spots, back.reshape(HELD, ROWS, LANES))

    def dense(results, held, flat, places, spots, routes):
        outgoing = packed(places, flat, SLOTS_ALL)
        arrived = by_plane(lax.all_to_all(outgoing.reshape(PEERS, 64, LANES), ALL, 0, 0, tiled=True))
        returned = lax.all_to_all(by_mesh(results.reshape(PEERS, 64, LANES)), ALL, 0, 0, tiled=True)
        return arrived.reshape(BLOCKS.shape), unpacked(places, returned.reshape(BLOCKS.shape))

    arrived, ks_blocks = lax.cond(over, dense, fast, results, held, flat, places, spots, routes)

    grid_rows = pl.pallas_call(
        grid_kernel,
        out_shape=jax.ShapeDtypeStruct((TASKS, 1, POINTS), jnp.float32),
        grid=(TASKS,),
        in_specs=[SMEM, whole(BLOCKS.shape), pl.BlockSpec((1, BASIS, POINTS), lambda t: (t, 0, 0))],
        out_specs=pl.BlockSpec((1, 1, POINTS), lambda t: (t, 0, 0)),
        scratch_shapes=[
            pltpu.VMEM((SLOTS_ALL + 1, ROWS, LANES), jnp.float32),
            pltpu.VMEM((BASIS, BASIS), jnp.bfloat16),
        ],
        compiler_params=params(),
        cost_estimate=pl.CostEstimate(flops=2 * TASKS * BASIS * BASIS * POINTS, bytes_accessed=14 << 20, transcendentals=0),
        name="collocate",
    )(labels, arrived, phi)
    density_grid = grid_rows.reshape(32, 1, 256)
    return density_grid, ks_blocks.reshape(atoms_here, offsets, BF, BF), margin_product


def solution(mesh):
    placed = (
        P(ALL, None, None, None),
        P(ALL, None, None, None),
        P("row", None, "col"),
        P(ALL, None, None, None),
        P(ALL, None, None),
        P(ALL, None),
        P(ALL, None, None),
    )
    return jax.shard_map(
        local,
        mesh=mesh,
        in_specs=placed,
        out_specs=(P(None, "row", "col"), P(ALL, None, None, None), P(ALL, None, None, None)),
        check_vma=False,
    )
```

```python
import functools

import jax
import jax.numpy as jnp
from jax import lax
from jax.experimental import pallas as pl
from jax.experimental.pallas import tpu as pltpu
from jax.sharding import PartitionSpec as P

HALF = 2
PAIRS = 120
PEERS = 256
SLOTS_ALL = 512
ROWS = 32
LANES = 128
BF = 64
TASKS = 8
BASIS = 512
POINTS = 1024
ALL = ("row", "col")
ZS = 8
PLANE = 32
CAP = 32
HELD = ZS * CAP
MESH = pl.DeviceIdType.MESH
VMEM_LIMIT = 56 * 1024 * 1024


def padded(array, sides, width):
    for axis, dim in sides:
        size, length = (lax.axis_size(axis), array.shape[dim])
        up = [(i, (i + 1) % size) for i in range(size)]
        down = [(j, i) for i, j in up]
        last = lax.slice_in_dim(array, length - width, length, axis=dim)
        first = lax.slice_in_dim(array, 0, width, axis=dim)
        before = lax.ppermute(last, axis, up)
        after = lax.ppermute(first, axis, down)
        array = jnp.concatenate([before, array, after], axis=dim)
    return array


def margin_of(density, margin):
    atoms_here = density.shape[0]
    offsets = density.shape[1]
    extended = padded(margin, ((ALL, 0),), HALF)
    columns = []
    for offset in range(offsets):
        lowest = max(0, offset - HALF)
        highest = min(offsets - 1, offset + HALF)
        left_blocks = density[:, lowest : highest + 1]
        right_blocks = jnp.stack(
            [extended[middle : middle + atoms_here, offset - middle + HALF] for middle in range(lowest, highest + 1)],
            axis=1,
        )
        columns.append(jnp.einsum("amik,amkj->aij", left_blocks, right_blocks, preferred_element_type=jnp.float32))
    return jnp.stack(columns, axis=1).astype(jnp.bfloat16)


def pack_kernel(place, density, out):
    def body(step, carry):
        for inner in range(8):
            pair = step * 8 + inner
            block = density[pair]
            spot = place[pair]
            out[spot, :, 0:BF] = block[0:ROWS]
            out[spot, :, BF:LANES] = block[ROWS:BF]
        return carry

    lax.fori_loop(0, PAIRS // 8, body, 0)


PSTEPS = [
    (dy, dx, dc)
    for dy, dx in (
        (2, 2), (1, 3), (3, 1), (1, 1), (3, 3), (2, 1), (2, 3), (1, 2), (3, 2), (0, 2), (2, 0), (0, 1), (0, 3), (1, 0), (3, 0), (0, 0),
    )
    for dc in (0, 1)
    if (dy, dx, dc) != (0, 0, 0)
]
ZSTEPS = (4, 3, 5, 2, 6, 1, 7)
WIDE = 640


def exchange_kernel(
    inverse, routes, held, results, density, margin, arrived, back, product,
    zgot, pgot, zput, pput, dens, marg, even, odd, zs, zr, ps, pr, zs2, zr2, ps2, pr2, hs, hr, own,
):
    row, col = lax.axis_index("row"), lax.axis_index("col")
    y, x, high = row // 8, lax.rem(row // 2, 4), lax.rem(row, 2)
    low, core = col // 2, lax.rem(col, 2)
    z = high * 4 + low
    here = (y * 4 + x) * 2 + core
    flat = row * 8 + col
    after, before = lax.rem(flat + 1, PEERS), lax.rem(flat + PEERS - 1, PEERS)
    after, before = (after // 8, lax.rem(after, 8)), (before // 8, lax.rem(before, 8))

    def along(step):
        to = lax.rem(z + step, ZS)
        return to, (y * 8 + x * 2 + to // 4, lax.rem(to, 4) * 2 + core)

    def across(steps):
        dy, dx, dc = steps
        to_y, to_x, to_c = lax.rem(y + dy, 4), lax.rem(x + dx, 4), lax.rem(core + dc, 2)
        return (to_y * 4 + to_x) * 2 + to_c, (to_y * 8 + to_x * 2 + high, low * 2 + to_c)

    def send(source, target, sent, received, where):
        copy = pltpu.make_async_remote_copy(
            src_ref=source, dst_ref=target, send_sem=sent, recv_sem=received, device_id=where, device_id_type=MESH
        )
        copy.start()
        return copy

    def keep(source, target, semaphore):
        copy = pltpu.make_async_copy(source, target, semaphore)
        copy.start()
        return copy

    def rows(ref, start, count):
        return ref.at[pl.ds(start * count, count)]

    barrier = pltpu.get_barrier_semaphore()
    for step in ZSTEPS:
        pl.semaphore_signal(barrier, inc=1, device_id=along(step)[1], device_id_type=MESH)
    for steps in PSTEPS:
        pl.semaphore_signal(barrier, inc=1, device_id=across(steps)[1], device_id_type=MESH)
    for where in (after, before):
        pl.semaphore_signal(barrier, inc=1, device_id=where, device_id_type=MESH)
    loads = [keep(density, dens, own.at[0]), keep(margin, marg.at[pl.ds(2, 24)], own.at[1])]
    pl.semaphore_wait(barrier, len(ZSTEPS) + len(PSTEPS) + 2)

    halos = [
        send(margin.at[pl.ds(22, 2)], marg.at[pl.ds(0, 2)], hs.at[0], hr.at[0], after),
        send(margin.at[pl.ds(0, 2)], marg.at[pl.ds(26, 2)], hs.at[1], hr.at[1], before),
    ]
    first_z, first_p = [], []
    for number in range(len(PSTEPS)):
        if number < len(ZSTEPS):
            to, where = along(ZSTEPS[number])
            first_z.append(send(rows(held, to, CAP), rows(zgot, z, CAP), zs.at[number], zr.at[number], where))
        to, where = across(PSTEPS[number])
        first_p.append(send(rows(results, to, 16), rows(pgot, here, 16), ps.at[number], pr.at[number], where))
    own_z = keep(rows(held, z, CAP), rows(zgot, z, CAP), own.at[2])
    own_p = keep(rows(results, here, 16), rows(pgot, here, 16), own.at[3])

    def clear(atom, carry):
        even[atom] = jnp.zeros((BF, WIDE), jnp.bfloat16)
        odd[atom] = jnp.zeros((BF, WIDE), jnp.bfloat16)
        return carry

    lax.fori_loop(0, 28, clear, 0)
    for copy in loads + halos:
        copy.wait()

    def widen(atom, carry):
        for block in range(5):
            piece = marg[atom, block]
            even[atom, :, (block + 2) * BF : (block + 3) * BF] = piece
            odd[atom, :, (block + 1) * BF : (block + 2) * BF] = piece
        return carry

    lax.fori_loop(0, 28, widen, 0)

    def multiply(atom, carry):
        total = jnp.zeros((BF, 384), jnp.float32)
        for middle in range(5):
            wide = even if middle % 2 == 0 else odd
            start = (4 - middle) // 2 * LANES
            total = total + jnp.dot(
                dens[atom, middle], wide[atom + middle, :, start : start + 384], preferred_element_type=jnp.float32
            )
        product[atom] = total.astype(jnp.bfloat16)
        return carry

    lax.fori_loop(0, 24, multiply, 0)

    for copy in first_z:
        copy.wait()
    own_z.wait()

    def gather_owner(to):
        def body(step, carry):
            for inner in range(8):
                spot = to * 16 + step * 8 + inner
                pput[spot] = zgot[inverse[spot]]
            return carry

        lax.fori_loop(0, 2, body, 0)

    def owner(number):
        to, where = across(PSTEPS[number])
        return send(rows(pput, to, 16), rows(arrived, here, 16), ps2.at[number], pr2.at[number], where)

    second = []
    gather_owner(across(PSTEPS[0])[0])
    for number in range(1, len(PSTEPS)):
        gather_owner(across(PSTEPS[number])[0])
        second.append(owner(number - 1))
    gather_owner(here)
    second.append(owner(len(PSTEPS) - 1))

    for copy in first_p:
        copy.wait()
    own_p.wait()

    def gather_holder(to):
        def body(step, carry):
            for inner in range(8):
                spot = to * CAP + step * 8 + inner
                zput[spot] = pgot[routes[spot]]
            return carry

        lax.fori_loop(0, CAP // 8, body, 0)

    def holder(number):
        to, where = along(ZSTEPS[number])
        return send(rows(zput, to, CAP), rows(back, z, CAP), zs2.at[number], zr2.at[number], where)

    gather_holder(along(ZSTEPS[0])[0])
    for number in range(1, len(ZSTEPS)):
        gather_holder(along(ZSTEPS[number])[0])
        second.append(holder(number - 1))
    gather_holder(z)
    second.append(holder(len(ZSTEPS) - 1))
    second.append(keep(rows(pput, here, 16), rows(arrived, here, 16), own.at[4]))
    second.append(keep(rows(zput, z, CAP), rows(back, z, CAP), own.at[5]))
    for copy in second:
        copy.wait()


def exchanged(inverse, routes, held, results, density, margin):
    hbm = pl.BlockSpec(memory_space=pl.ANY)
    dma = pltpu.SemaphoreType.DMA
    return pl.pallas_call(
        exchange_kernel,
        out_shape=(
            BLOCKS,
            jax.ShapeDtypeStruct((HELD, ROWS, LANES), jnp.bfloat16),
            jax.ShapeDtypeStruct((24, BF, 384), jnp.bfloat16),
        ),
        in_specs=[SMEM, SMEM, hbm, hbm, hbm, hbm],
        out_specs=(hbm, hbm, VM),
        scratch_shapes=[
            pltpu.VMEM((HELD, ROWS, LANES), jnp.bfloat16),
            pltpu.VMEM((SLOTS_ALL, ROWS, LANES), jnp.bfloat16),
            pltpu.VMEM((HELD, ROWS, LANES), jnp.bfloat16),
            pltpu.VMEM((SLOTS_ALL, ROWS, LANES), jnp.bfloat16),
            pltpu.VMEM((24, 5, BF, BF), jnp.bfloat16),
            pltpu.VMEM((28, 5, BF, BF), jnp.bfloat16),
            pltpu.VMEM((28, BF, WIDE), jnp.bfloat16),
            pltpu.VMEM((28, BF, WIDE), jnp.bfloat16),
            dma((7,)), dma((7,)), dma((31,)), dma((31,)),
            dma((7,)), dma((7,)), dma((31,)), dma((31,)),
            dma((2,)), dma((2,)), dma((6,)),
        ],
        compiler_params=params(collective_id=0, has_side_effects=True),
        name="exchange",
    )(inverse, routes, held, results, density, margin)


def matrix_kernel(label, basis, potential, out, scaled, table):
    task = pl.program_id(0)
    phi = basis[0]
    scaled[...] = (phi.astype(jnp.float32) * potential[0]).astype(jnp.bfloat16)
    full = lax.dot_general(
        scaled[...], phi, (((1,), (1,)), ((), ())), preferred_element_type=jnp.float32
    )
    left = lax.broadcasted_iota(jnp.int32, (ROWS, LANES), 1) < BF
    for first in range(8):
        for pair in range(4):
            columns = slice(pair * LANES, (pair + 1) * LANES)
            top = full[first * BF : first * BF + ROWS, columns]
            low = full[first * BF + ROWS : (first + 1) * BF, columns]
            spot = task * 64 + first * 8 + 2 * pair
            table[spot] = jnp.where(left, top, pltpu.roll(low, BF, 1)).astype(jnp.bfloat16)
            table[spot + 1] = jnp.where(left, pltpu.roll(top, BF, 1), low).astype(jnp.bfloat16)

    @pl.when(task == TASKS - 1)
    def _():
        def body(step, carry):
            for inner in range(16):
                slot = step * 16 + inner
                out[slot] = table[jnp.maximum(label[slot], 0)]
            return carry

        lax.fori_loop(0, SLOTS_ALL // 16, body, 0)


def grid_kernel(label, place, blocks, basis, back, product, out, ks, margins, table, weights):
    task = pl.program_id(0)

    @pl.when(task == 0)
    def _():
        def clear(step, carry):
            for inner in range(8):
                table[step * 8 + inner] = jnp.zeros((ROWS, LANES), jnp.float32)
            return carry

        lax.fori_loop(0, SLOTS_ALL // 8, clear, 0)

        def body(step, carry):
            for inner in range(8):
                slot = step * 8 + inner
                which = label[slot]
                spot = jnp.where(which < 0, SLOTS_ALL, which)
                table[spot] = table[spot] + blocks[slot].astype(jnp.float32)
            return carry

        lax.fori_loop(0, SLOTS_ALL // 8, body, 0)

    left = lax.broadcasted_iota(jnp.int32, (ROWS, LANES), 1) < BF
    for first in range(8):
        for pair in range(4):
            spot = task * 64 + first * 8 + 2 * pair
            one = table[spot]
            two = table[spot + 1]
            columns = slice(pair * LANES, (pair + 1) * LANES)
            weights[first * BF : first * BF + ROWS, columns] = jnp.where(left, one, pltpu.roll(two, BF, 1)).astype(
                jnp.bfloat16
            )
            weights[first * BF + ROWS : (first + 1) * BF, columns] = jnp.where(left, pltpu.roll(one, BF, 1), two).astype(
                jnp.bfloat16
            )
    for piece in range(4):
        columns = slice(piece * 256, (piece + 1) * 256)
        phi = basis[0, :, columns]
        weighted = jnp.dot(weights[...], phi, preferred_element_type=jnp.float32)
        out[0, :, columns] = jnp.sum(phi.astype(jnp.float32) * weighted, axis=0, keepdims=True)
    for pair in range(15):
        block = back[place[task * 15 + pair]]
        ks[pair, 0:ROWS] = block[:, 0:BF]
        ks[pair, ROWS:BF] = block[:, BF:LANES]
    for atom in range(3):
        for offset in range(5):
            margins[atom * 5 + offset] = product[atom, :, offset * BF : (offset + 1) * BF]


def params(**more):
    return pltpu.CompilerParams(vmem_limit_bytes=VMEM_LIMIT, **more)


SMEM = pl.BlockSpec(memory_space=pltpu.SMEM)
VM = pl.BlockSpec(memory_space=pltpu.VMEM)
BLOCKS = jax.ShapeDtypeStruct((SLOTS_ALL, ROWS, LANES), jnp.bfloat16)


def whole(shape):
    return pl.BlockSpec(shape, lambda *_: (0,) * len(shape))


def packed(places, flat, blocks):
    return pl.pallas_call(
        pack_kernel,
        out_shape=jax.ShapeDtypeStruct((blocks, ROWS, LANES), jnp.bfloat16),
        in_specs=[SMEM, VM],
        out_specs=VM,
        compiler_params=params(),
        cost_estimate=pl.CostEstimate(flops=0, bytes_accessed=6 << 20, transcendentals=0),
        name="pack",
    )(places, flat)


def by_plane(values):
    rest = values.shape[1:]
    return values.reshape((16, 8, 2) + rest).swapaxes(1, 2).reshape((PEERS,) + rest)


def by_mesh(values):
    rest = values.shape[1:]
    return values.reshape((16, 2, 8) + rest).swapaxes(1, 2).reshape((PEERS,) + rest)


def local(density, margin, potential, basis_values, pair_owner, pair_box, pair_slots):
    atoms_here, offsets = density.shape[:2]
    row, col = lax.axis_index("row"), lax.axis_index("col")
    owners = pair_owner.reshape(PAIRS)
    planes = (owners // 8) % 2 * 4 + owners % 8 // 2
    inside = owners // 16 * 2 + owners % 2
    before = jnp.arange(PAIRS)[:, None] > jnp.arange(PAIRS)[None, :]
    ranks = jnp.sum(((owners[:, None] == owners[None, :]) & before).astype(jnp.int32), axis=1)
    turns = jnp.sum(((planes[:, None] == planes[None, :]) & before).astype(jnp.int32), axis=1)
    places = owners * 2 + ranks
    spots = jnp.where(turns < CAP, planes * CAP + turns, HELD)
    flat = density.reshape(PAIRS, BF, BF)
    held = packed(spots, flat, HELD + CAP)

    fields = jnp.stack(
        [pair_box.reshape(PAIRS), pair_slots[..., 0].reshape(PAIRS), pair_slots[..., 1].reshape(PAIRS)], axis=0
    )
    chosen = jnp.arange(SLOTS_ALL, dtype=jnp.int32)[None, :, None] == places[None, None, :]
    tags = jnp.sum(jnp.where(chosen, fields[:, None, :] + 1, 0), axis=2) - 1
    tags = tags.reshape(3, PEERS, 2).transpose(1, 0, 2).reshape(PEERS, 6)
    listed = jnp.arange(HELD, dtype=jnp.int32)[:, None] == spots[None, :]
    targets = jnp.sum(jnp.where(listed, (inside * 2 + ranks)[None, :] + 1, 0), axis=1) - 1
    targets = jnp.broadcast_to(targets.reshape(1, ZS, 1, CAP), (16, ZS, 2, CAP)).reshape(PEERS, CAP)
    over = jnp.max(turns) >= CAP
    rows = jnp.broadcast_to(potential[0][:, None, :], (32, 8, 256)).reshape(PEERS, 256)
    notes = jnp.concatenate(
        [tags, jnp.broadcast_to(over.astype(jnp.int32), (PEERS, 2)), targets, jnp.zeros((PEERS, LANES - 8 - CAP), jnp.int32)],
        axis=1,
    ).astype(jnp.float32)
    sent = jnp.concatenate([notes, rows], axis=1).reshape(PEERS, 1, LANES + 256)
    got = lax.all_to_all(sent, ALL, 0, 0, tiled=True).reshape(PEERS, LANES + 256)
    notes = got[:, :LANES].astype(jnp.int32)
    pencil = lax.dynamic_index_in_dim(got[:, LANES:].reshape(32, 8, 256), col, 1, keepdims=False)
    box_potential = pencil.reshape(TASKS, 1, POINTS)
    over = jnp.max(notes[:, 6]) > 0
    tags = by_plane(notes[:, :6]).reshape(PEERS, 3, 2)
    labels = jnp.where(tags[:, 0] < 0, -1, tags[:, 0] * 64 + tags[:, 1] * 8 + tags[:, 2]).reshape(SLOTS_ALL)
    here = row // 2 * 2 + col % 2
    targets = lax.dynamic_index_in_dim(by_plane(notes[:, 8 : 8 + CAP]).reshape(PLANE, ZS, CAP), here, 0, keepdims=False)
    number = jnp.arange(HELD, dtype=jnp.int32)
    targets = targets.reshape(HELD)
    routes = targets // 2 * 16 + number // CAP * 2 + targets % 2
    inverse = jnp.sum(
        jnp.where(
            (jnp.arange(SLOTS_ALL, dtype=jnp.int32)[:, None] == routes[None, :]) & (targets >= 0)[None, :], number[None, :], 0
        ),
        axis=1,
    )
    routes = jnp.where(targets < 0, 0, routes)

    phi = basis_values.reshape(TASKS, BASIS, POINTS)
    results = pl.pallas_call(
        matrix_kernel,
        out_shape=BLOCKS,
        grid=(TASKS,),
        in_specs=[
            SMEM,
            pl.BlockSpec((1, BASIS, POINTS), lambda t: (t, 0, 0)),
            pl.BlockSpec((1, 1, POINTS), lambda t: (t, 0, 0)),
        ],
        out_specs=whole(BLOCKS.shape),
        scratch_shapes=[
            pltpu.VMEM((BASIS, POINTS), jnp.bfloat16),
            pltpu.VMEM((SLOTS_ALL, ROWS, LANES), jnp.bfloat16),
        ],
        compiler_params=params(),
        cost_estimate=pl.CostEstimate(flops=2 * TASKS * BASIS * BASIS * POINTS, bytes_accessed=14 << 20, transcendentals=0),
        name="matrices",
    )(labels, phi, box_potential)

    def fast(results, held, density, margin, places, routes, inverse):
        return exchanged(inverse, routes, held, results, density, margin)

    def dense(results, held, density, margin, places, routes, inverse):
        outgoing = packed(places, density.reshape(PAIRS, BF, BF), SLOTS_ALL)
        arrived = by_plane(lax.all_to_all(outgoing.reshape(PEERS, 64, LANES), ALL, 0, 0, tiled=True))
        returned = lax.all_to_all(by_mesh(results.reshape(PEERS, 64, LANES)), ALL, 0, 0, tiled=True)
        back = returned.reshape(BLOCKS.shape)[places]
        wide = margin_of(density, margin).transpose(0, 2, 1, 3).reshape(atoms_here, BF, offsets * BF)
        return (
            arrived.reshape(BLOCKS.shape),
            jnp.pad(back, ((0, HELD - PAIRS), (0, 0), (0, 0))),
            jnp.pad(wide, ((0, 0), (0, 0), (0, BF))),
        )

    arrived, back, product = lax.cond(over, dense, fast, results, held, density, margin, places, routes, inverse)
    pickup = jnp.where(over, jnp.arange(PAIRS, dtype=jnp.int32), spots)

    grid_rows, ks_blocks, margin_product = pl.pallas_call(
        grid_kernel,
        out_shape=(
            jax.ShapeDtypeStruct((TASKS, 1, POINTS), jnp.float32),
            jax.ShapeDtypeStruct((PAIRS, BF, BF), jnp.bfloat16),
            jax.ShapeDtypeStruct((PAIRS, BF, BF), jnp.bfloat16),
        ),
        grid=(TASKS,),
        in_specs=[
            SMEM,
            SMEM,
            whole(BLOCKS.shape),
            pl.BlockSpec((1, BASIS, POINTS), lambda t: (t, 0, 0)),
            whole((HELD, ROWS, LANES)),
            pl.BlockSpec((3, BF, 384), lambda t: (t, 0, 0)),
        ],
        out_specs=(
            pl.BlockSpec((1, 1, POINTS), lambda t: (t, 0, 0)),
            pl.BlockSpec((15, BF, BF), lambda t: (t, 0, 0)),
            pl.BlockSpec((15, BF, BF), lambda t: (t, 0, 0)),
        ),
        scratch_shapes=[
            pltpu.VMEM((SLOTS_ALL + 1, ROWS, LANES), jnp.float32),
            pltpu.VMEM((BASIS, BASIS), jnp.bfloat16),
        ],
        compiler_params=params(),
        name="collocate",
    )(labels, pickup, arrived, phi, back, product)
    density_grid = grid_rows.reshape(32, 1, 256)
    return density_grid, ks_blocks.reshape(atoms_here, offsets, BF, BF), margin_product.reshape(atoms_here, offsets, BF, BF)


def solution(mesh):
    placed = (
        P(ALL, None, None, None),
        P(ALL, None, None, None),
        P("row", None, "col"),
        P(ALL, None, None, None),
        P(ALL, None, None),
        P(ALL, None),
        P(ALL, None, None),
    )
    return jax.shard_map(
        local,
        mesh=mesh,
        in_specs=placed,
        out_specs=(P(None, "row", "col"), P(ALL, None, None, None), P(ALL, None, None, None)),
        check_vma=False,
    )
```

```python
import functools

import jax
import jax.numpy as jnp
from jax import lax
from jax.experimental import pallas as pl
from jax.experimental.pallas import tpu as pltpu
from jax.sharding import PartitionSpec as P

HALF = 2
PAIRS = 120
PEERS = 256
SLOTS_ALL = 512
ROWS = 32
LANES = 128
BF = 64
TASKS = 8
BASIS = 512
POINTS = 1024
ALL = ("row", "col")
ZS = 8
PLANE = 32
CAP = 28
HELD = ZS * CAP
MESH = pl.DeviceIdType.MESH
VMEM_LIMIT = 56 * 1024 * 1024


def padded(array, sides, width):
    for axis, dim in sides:
        size, length = (lax.axis_size(axis), array.shape[dim])
        up = [(i, (i + 1) % size) for i in range(size)]
        down = [(j, i) for i, j in up]
        last = lax.slice_in_dim(array, length - width, length, axis=dim)
        first = lax.slice_in_dim(array, 0, width, axis=dim)
        before = lax.ppermute(last, axis, up)
        after = lax.ppermute(first, axis, down)
        array = jnp.concatenate([before, array, after], axis=dim)
    return array


def margin_of(density, margin):
    atoms_here = density.shape[0]
    offsets = density.shape[1]
    extended = padded(margin, ((ALL, 0),), HALF)
    columns = []
    for offset in range(offsets):
        lowest = max(0, offset - HALF)
        highest = min(offsets - 1, offset + HALF)
        left_blocks = density[:, lowest : highest + 1]
        right_blocks = jnp.stack(
            [extended[middle : middle + atoms_here, offset - middle + HALF] for middle in range(lowest, highest + 1)],
            axis=1,
        )
        columns.append(jnp.einsum("amik,amkj->aij", left_blocks, right_blocks, preferred_element_type=jnp.float32))
    return jnp.stack(columns, axis=1).astype(jnp.bfloat16)


def pack_kernel(place, density, out):
    def body(step, carry):
        for inner in range(8):
            pair = step * 8 + inner
            block = density[pair]
            spot = place[pair]
            out[spot, :, 0:BF] = block[0:ROWS]
            out[spot, :, BF:LANES] = block[ROWS:BF]
        return carry

    lax.fori_loop(0, PAIRS // 8, body, 0)


PSTEPS = [
    (dy, dx, dc)
    for dy, dx in (
        (2, 2), (1, 3), (3, 1), (1, 1), (3, 3), (2, 1), (2, 3), (1, 2), (3, 2), (0, 2), (2, 0), (0, 1), (0, 3), (1, 0), (3, 0), (0, 0),
    )
    for dc in (0, 1)
    if (dy, dx, dc) != (0, 0, 0)
]
ZSTEPS = (4, 3, 5, 2, 6, 1, 7)
WIDE = 640


def exchange_kernel(
    inverse, routes, held, results, density, margin, arrived, back, product,
    zgot, pgot, zput, pput, dens, marg, even, odd, zs, zr, ps, pr, zs2, zr2, ps2, pr2, hs, hr, own,
):
    row, col = lax.axis_index("row"), lax.axis_index("col")
    y, x, high = row // 8, lax.rem(row // 2, 4), lax.rem(row, 2)
    low, core = col // 2, lax.rem(col, 2)
    z = high * 4 + low
    here = (y * 4 + x) * 2 + core
    flat = row * 8 + col
    after, before = lax.rem(flat + 1, PEERS), lax.rem(flat + PEERS - 1, PEERS)
    after, before = (after // 8, lax.rem(after, 8)), (before // 8, lax.rem(before, 8))

    def along(step):
        to = lax.rem(z + step, ZS)
        return to, (y * 8 + x * 2 + to // 4, lax.rem(to, 4) * 2 + core)

    def across(steps):
        dy, dx, dc = steps
        to_y, to_x, to_c = lax.rem(y + dy, 4), lax.rem(x + dx, 4), lax.rem(core + dc, 2)
        return (to_y * 4 + to_x) * 2 + to_c, (to_y * 8 + to_x * 2 + high, low * 2 + to_c)

    def send(source, target, sent, received, where):
        copy = pltpu.make_async_remote_copy(
            src_ref=source, dst_ref=target, send_sem=sent, recv_sem=received, device_id=where, device_id_type=MESH
        )
        copy.start()
        return copy

    def keep(source, target, semaphore):
        copy = pltpu.make_async_copy(source, target, semaphore)
        copy.start()
        return copy

    def rows(ref, start, count):
        return ref.at[pl.ds(start * count, count)]

    barrier = pltpu.get_barrier_semaphore()
    for step in ZSTEPS:
        pl.semaphore_signal(barrier, inc=1, device_id=along(step)[1], device_id_type=MESH)
    for steps in PSTEPS:
        pl.semaphore_signal(barrier, inc=1, device_id=across(steps)[1], device_id_type=MESH)
    for where in (after, before):
        pl.semaphore_signal(barrier, inc=1, device_id=where, device_id_type=MESH)
    loads = [keep(density, dens, own.at[0]), keep(margin, marg.at[pl.ds(2, 24)], own.at[1])]
    pl.semaphore_wait(barrier, len(ZSTEPS) + len(PSTEPS) + 2)

    halos = [
        send(margin.at[pl.ds(22, 2)], marg.at[pl.ds(0, 2)], hs.at[0], hr.at[0], after),
        send(margin.at[pl.ds(0, 2)], marg.at[pl.ds(26, 2)], hs.at[1], hr.at[1], before),
    ]
    first_z, first_p = [], []
    for number in range(len(PSTEPS)):
        if number < len(ZSTEPS):
            to, where = along(ZSTEPS[number])
            first_z.append(send(rows(held, to, CAP), rows(zgot, z, CAP), zs.at[number], zr.at[number], where))
        to, where = across(PSTEPS[number])
        first_p.append(send(rows(results, to, 16), rows(pgot, here, 16), ps.at[number], pr.at[number], where))
    own_z = keep(rows(held, z, CAP), rows(zgot, z, CAP), own.at[2])
    own_p = keep(rows(results, here, 16), rows(pgot, here, 16), own.at[3])

    def clear(atom, carry):
        even[atom] = jnp.zeros((BF, WIDE), jnp.bfloat16)
        odd[atom] = jnp.zeros((BF, WIDE), jnp.bfloat16)
        return carry

    lax.fori_loop(0, 28, clear, 0)
    for copy in loads + halos:
        copy.wait()

    def widen(atom, carry):
        for block in range(5):
            piece = marg[atom, block]
            even[atom, :, (block + 2) * BF : (block + 3) * BF] = piece
            odd[atom, :, (block + 1) * BF : (block + 2) * BF] = piece
        return carry

    lax.fori_loop(0, 28, widen, 0)

    def multiply(atom, carry):
        total = jnp.zeros((BF, 384), jnp.float32)
        for middle in range(5):
            wide = even if middle % 2 == 0 else odd
            start = (4 - middle) // 2 * LANES
            total = total + jnp.dot(
                dens[atom, middle], wide[atom + middle, :, start : start + 384], preferred_element_type=jnp.float32
            )
        product[atom] = total.astype(jnp.bfloat16)
        return carry

    lax.fori_loop(0, 24, multiply, 0)

    for copy in first_z:
        copy.wait()
    own_z.wait()

    def gather_owner(to):
        def body(step, carry):
            for inner in range(8):
                spot = to * 16 + step * 8 + inner
                pput[spot] = zgot[inverse[spot]]
            return carry

        lax.fori_loop(0, 2, body, 0)

    def owner(number):
        to, where = across(PSTEPS[number])
        return send(rows(pput, to, 16), rows(arrived, here, 16), ps2.at[number], pr2.at[number], where)

    second = []
    gather_owner(across(PSTEPS[0])[0])
    for number in range(1, len(PSTEPS)):
        gather_owner(across(PSTEPS[number])[0])
        second.append(owner(number - 1))
    gather_owner(here)
    second.append(owner(len(PSTEPS) - 1))

    for copy in first_p:
        copy.wait()
    own_p.wait()

    def gather_holder(to):
        def body(step, carry):
            for inner in range(4):
                spot = to * CAP + step * 4 + inner
                zput[spot] = pgot[routes[spot]]
            return carry

        lax.fori_loop(0, CAP // 4, body, 0)

    def holder(number):
        to, where = along(ZSTEPS[number])
        return send(rows(zput, to, CAP), rows(back, z, CAP), zs2.at[number], zr2.at[number], where)

    gather_holder(along(ZSTEPS[0])[0])
    for number in range(1, len(ZSTEPS)):
        gather_holder(along(ZSTEPS[number])[0])
        second.append(holder(number - 1))
    gather_holder(z)
    second.append(holder(len(ZSTEPS) - 1))
    second.append(keep(rows(pput, here, 16), rows(arrived, here, 16), own.at[4]))
    second.append(keep(rows(zput, z, CAP), rows(back, z, CAP), own.at[5]))
    for copy in second:
        copy.wait()


def exchanged(inverse, routes, held, results, density, margin):
    hbm = pl.BlockSpec(memory_space=pl.ANY)
    dma = pltpu.SemaphoreType.DMA
    return pl.pallas_call(
        exchange_kernel,
        out_shape=(
            BLOCKS,
            jax.ShapeDtypeStruct((HELD, ROWS, LANES), jnp.bfloat16),
            jax.ShapeDtypeStruct((24, BF, 384), jnp.bfloat16),
        ),
        in_specs=[SMEM, SMEM, hbm, hbm, hbm, hbm],
        out_specs=(hbm, hbm, VM),
        scratch_shapes=[
            pltpu.VMEM((HELD, ROWS, LANES), jnp.bfloat16),
            pltpu.VMEM((SLOTS_ALL, ROWS, LANES), jnp.bfloat16),
            pltpu.VMEM((HELD, ROWS, LANES), jnp.bfloat16),
            pltpu.VMEM((SLOTS_ALL, ROWS, LANES), jnp.bfloat16),
            pltpu.VMEM((24, 5, BF, BF), jnp.bfloat16),
            pltpu.VMEM((28, 5, BF, BF), jnp.bfloat16),
            pltpu.VMEM((28, BF, WIDE), jnp.bfloat16),
            pltpu.VMEM((28, BF, WIDE), jnp.bfloat16),
            dma((7,)), dma((7,)), dma((31,)), dma((31,)),
            dma((7,)), dma((7,)), dma((31,)), dma((31,)),
            dma((2,)), dma((2,)), dma((6,)),
        ],
        compiler_params=params(collective_id=0, has_side_effects=True),
        name="exchange",
    )(inverse, routes, held, results, density, margin)


def notice_kernel(
    which, table, potential, density, got, pencil, held, zgot, other, zs, zr, ps, pr, qs, qr, us, ur, own
):
    row, col = lax.axis_index("row"), lax.axis_index("col")
    y, x, high = row // 8, lax.rem(row // 2, 4), lax.rem(row, 2)
    low, core = col // 2, lax.rem(col, 2)
    z = high * 4 + low
    here = (y * 4 + x) * 2 + core
    flipped = y * 8 + x * 2 + (1 - high)

    def along(step):
        to = lax.rem(z + step, ZS)
        return to, (y * 8 + x * 2 + to // 4, lax.rem(to, 4) * 2 + core)

    def across(steps):
        dy, dx, dc = steps
        to_y, to_x, to_c = lax.rem(y + dy, 4), lax.rem(x + dx, 4), lax.rem(core + dc, 2)
        return (to_y * 4 + to_x) * 2 + to_c, (to_y * 8 + to_x * 2 + high, low * 2 + to_c)

    def send(source, target, sent, received, where):
        copy = pltpu.make_async_remote_copy(
            src_ref=source, dst_ref=target, send_sem=sent, recv_sem=received, device_id=where, device_id_type=MESH
        )
        copy.start()
        return copy

    def keep(source, target, semaphore):
        copy = pltpu.make_async_copy(source, target, semaphore)
        copy.start()
        return copy

    barrier = pltpu.get_barrier_semaphore()
    for step in ZSTEPS:
        pl.semaphore_signal(barrier, inc=1, device_id=along(step)[1], device_id_type=MESH)
    for steps in PSTEPS:
        pl.semaphore_signal(barrier, inc=1, device_id=across(steps)[1], device_id_type=MESH)
    pl.semaphore_wait(barrier, len(ZSTEPS) + len(PSTEPS))

    first = [send(potential, other, zs.at[7], zr.at[7], along(4)[1])]
    for number in range(len(ZSTEPS)):
        to, where = along(ZSTEPS[number])
        first.append(send(table.at[to], zgot.at[z], zs.at[number], zr.at[number], where))
    first.append(keep(table.at[z], zgot.at[z], own.at[0]))

    def pack(step, carry):
        for inner in range(8):
            spot = step * 8 + inner
            block = density[which[spot]]
            held[spot, :, 0:BF] = block[0:ROWS]
            held[spot, :, BF:LANES] = block[ROWS:BF]
        return carry

    lax.fori_loop(0, HELD // 8, pack, 0)
    for copy in first:
        copy.wait()

    second, line = [], 0
    for number in range(len(PSTEPS)):
        to, where = across(PSTEPS[number])
        second.append(send(zgot.at[:, to], got.at[here], ps.at[number], pr.at[number], where))
        if PSTEPS[number][2] == 0:
            second.append(send(potential.at[where[0]], pencil.at[row], qs.at[line], qr.at[line], where))
            second.append(send(other.at[where[0]], pencil.at[flipped], us.at[line], ur.at[line], where))
            line += 1
    second.append(keep(zgot.at[:, here], got.at[here], own.at[1]))
    second.append(keep(potential.at[row], pencil.at[row], own.at[2]))
    second.append(keep(other.at[row], pencil.at[flipped], own.at[3]))
    for copy in second:
        copy.wait()


def noticed(which, table, potential, flat):
    dma = pltpu.SemaphoreType.DMA
    return pl.pallas_call(
        notice_kernel,
        out_shape=(
            jax.ShapeDtypeStruct((PLANE, ZS, 1, LANES), jnp.int32),
            jax.ShapeDtypeStruct((32, 1, 256), jnp.float32),
            jax.ShapeDtypeStruct((HELD, ROWS, LANES), jnp.bfloat16),
        ),
        in_specs=[SMEM, VM, VM, VM],
        out_specs=(VM, VM, VM),
        scratch_shapes=[
            pltpu.VMEM((ZS, PLANE, 1, LANES), jnp.int32),
            pltpu.VMEM((32, 1, 256), jnp.float32),
            dma((8,)), dma((8,)), dma((31,)), dma((31,)), dma((15,)), dma((15,)), dma((15,)), dma((15,)), dma((4,)),
        ],
        compiler_params=params(collective_id=1, has_side_effects=True),
        name="notices",
    )(which, table, potential, flat)


def matrix_kernel(label, basis, potential, out, scaled, table):
    task = pl.program_id(0)
    phi = basis[0]
    scaled[...] = (phi.astype(jnp.float32) * potential[0]).astype(jnp.bfloat16)
    full = lax.dot_general(
        scaled[...], phi, (((1,), (1,)), ((), ())), preferred_element_type=jnp.float32
    )
    left = lax.broadcasted_iota(jnp.int32, (ROWS, LANES), 1) < BF
    for first in range(8):
        for pair in range(4):
            columns = slice(pair * LANES, (pair + 1) * LANES)
            top = full[first * BF : first * BF + ROWS, columns]
            low = full[first * BF + ROWS : (first + 1) * BF, columns]
            spot = task * 64 + first * 8 + 2 * pair
            table[spot] = jnp.where(left, top, pltpu.roll(low, BF, 1)).astype(jnp.bfloat16)
            table[spot + 1] = jnp.where(left, pltpu.roll(top, BF, 1), low).astype(jnp.bfloat16)

    @pl.when(task == TASKS - 1)
    def _():
        def body(step, carry):
            for inner in range(16):
                slot = step * 16 + inner
                out[slot] = table[jnp.maximum(label[slot], 0)]
            return carry

        lax.fori_loop(0, SLOTS_ALL // 16, body, 0)


def grid_kernel(label, place, blocks, basis, back, product, out, ks, margins, table, weights):
    task = pl.program_id(0)

    @pl.when(task == 0)
    def _():
        def clear(step, carry):
            for inner in range(8):
                table[step * 8 + inner] = jnp.zeros((ROWS, LANES), jnp.float32)
            return carry

        lax.fori_loop(0, SLOTS_ALL // 8, clear, 0)

        def body(step, carry):
            for inner in range(8):
                slot = step * 8 + inner
                which = label[slot]
                spot = jnp.where(which < 0, SLOTS_ALL, which)
                table[spot] = table[spot] + blocks[slot].astype(jnp.float32)
            return carry

        lax.fori_loop(0, SLOTS_ALL // 8, body, 0)

    left = lax.broadcasted_iota(jnp.int32, (ROWS, LANES), 1) < BF
    for first in range(8):
        for pair in range(4):
            spot = task * 64 + first * 8 + 2 * pair
            one = table[spot]
            two = table[spot + 1]
            columns = slice(pair * LANES, (pair + 1) * LANES)
            weights[first * BF : first * BF + ROWS, columns] = jnp.where(left, one, pltpu.roll(two, BF, 1)).astype(
                jnp.bfloat16
            )
            weights[first * BF + ROWS : (first + 1) * BF, columns] = jnp.where(left, pltpu.roll(one, BF, 1), two).astype(
                jnp.bfloat16
            )
    for piece in range(4):
        columns = slice(piece * 256, (piece + 1) * 256)
        phi = basis[0, :, columns]
        weighted = jnp.dot(weights[...], phi, preferred_element_type=jnp.float32)
        out[0, :, columns] = jnp.sum(phi.astype(jnp.float32) * weighted, axis=0, keepdims=True)
    for pair in range(15):
        block = back[place[task * 15 + pair]]
        ks[pair, 0:ROWS] = block[:, 0:BF]
        ks[pair, ROWS:BF] = block[:, BF:LANES]
    for atom in range(3):
        for offset in range(5):
            margins[atom * 5 + offset] = product[atom, :, offset * BF : (offset + 1) * BF]


def params(**more):
    return pltpu.CompilerParams(vmem_limit_bytes=VMEM_LIMIT, **more)


SMEM = pl.BlockSpec(memory_space=pltpu.SMEM)
VM = pl.BlockSpec(memory_space=pltpu.VMEM)
BLOCKS = jax.ShapeDtypeStruct((SLOTS_ALL, ROWS, LANES), jnp.bfloat16)


def whole(shape):
    return pl.BlockSpec(shape, lambda *_: (0,) * len(shape))


def packed(places, flat, blocks):
    return pl.pallas_call(
        pack_kernel,
        out_shape=jax.ShapeDtypeStruct((blocks, ROWS, LANES), jnp.bfloat16),
        in_specs=[SMEM, VM],
        out_specs=VM,
        compiler_params=params(),
        cost_estimate=pl.CostEstimate(flops=0, bytes_accessed=6 << 20, transcendentals=0),
        name="pack",
    )(places, flat)


def by_plane(values):
    rest = values.shape[1:]
    return values.reshape((16, 8, 2) + rest).swapaxes(1, 2).reshape((PEERS,) + rest)


def by_mesh(values):
    rest = values.shape[1:]
    return values.reshape((16, 2, 8) + rest).swapaxes(1, 2).reshape((PEERS,) + rest)


def local(density, margin, potential, basis_values, pair_owner, pair_box, pair_slots):
    atoms_here, offsets = density.shape[:2]
    row, col = lax.axis_index("row"), lax.axis_index("col")
    owners = pair_owner.reshape(PAIRS)
    planes = (owners // 8) % 2 * 4 + owners % 8 // 2
    inside = owners // 16 * 2 + owners % 2
    order = jnp.arange(PAIRS, dtype=jnp.int32)
    before = order[:, None] > order[None, :]
    ranks = jnp.sum(((owners[:, None] == owners[None, :]) & before).astype(jnp.int32), axis=1)
    turns = jnp.sum(((planes[:, None] == planes[None, :]) & before).astype(jnp.int32), axis=1)
    places = owners * 2 + ranks
    spots = jnp.where(turns < CAP, planes * CAP + turns, HELD)
    flat = density.reshape(PAIRS, BF, BF)
    which = jnp.sum(
        jnp.where(jnp.arange(HELD, dtype=jnp.int32)[:, None] == spots[None, :], order[None, :], 0), axis=1
    )
    over = jnp.max(turns) >= CAP
    lanes = jnp.arange(LANES, dtype=jnp.int32)[None, :]
    peers = jnp.arange(PEERS, dtype=jnp.int32)[:, None]

    def column(values):
        return values.reshape(PAIRS, 1)

    box, one, two = column(pair_box), column(pair_slots[..., 0]), column(pair_slots[..., 1])
    field = jnp.where(lanes < 2, box, jnp.where(lanes < 4, one, two)) + 1
    to_owner = jnp.where((lanes < 6) & (lanes % 2 == column(ranks)), field, 0)
    to_plane = jnp.where(lanes - 8 == column(turns), column(inside * 2 + ranks) + 1, 0)
    at_owner = peers == (planes * PLANE + inside)[None, :]
    at_plane = peers // PLANE == planes[None, :]

    def listed(chosen, values):
        return jnp.dot(chosen.astype(jnp.bfloat16), values.astype(jnp.bfloat16), preferred_element_type=jnp.float32)

    table = (listed(at_owner, to_owner) + listed(at_plane, to_plane)).astype(jnp.int32) - 1
    table = jnp.where(lanes == 6, over.astype(jnp.int32), table)
    got, pencil, held = noticed(
        which, table.reshape(ZS, PLANE, 1, LANES), potential.reshape(32, 1, 256), flat
    )
    box_potential = pencil.reshape(TASKS, 1, POINTS)
    got = got.reshape(PEERS, LANES)
    over = jnp.max(got[:, 6]) > 0
    tags = got[:, 0:2] * 64 + got[:, 2:4] * 8 + got[:, 4:6]
    labels = jnp.where(got[:, 0:2] < 0, -1, tags).reshape(SLOTS_ALL)
    here = row // 2 * 2 + col % 2
    targets = lax.dynamic_slice(got, (here * ZS, 8), (ZS, CAP))
    number = jnp.arange(HELD, dtype=jnp.int32)
    targets = targets.reshape(HELD)
    routes = targets // 2 * 16 + number // CAP * 2 + targets % 2
    inverse = jnp.sum(
        jnp.where(
            (jnp.arange(SLOTS_ALL, dtype=jnp.int32)[:, None] == routes[None, :]) & (targets >= 0)[None, :], number[None, :], 0
        ),
        axis=1,
    )
    routes = jnp.where(targets < 0, 0, routes)

    phi = basis_values.reshape(TASKS, BASIS, POINTS)
    results = pl.pallas_call(
        matrix_kernel,
        out_shape=BLOCKS,
        grid=(TASKS,),
        in_specs=[
            SMEM,
            pl.BlockSpec((1, BASIS, POINTS), lambda t: (t, 0, 0)),
            pl.BlockSpec((1, 1, POINTS), lambda t: (t, 0, 0)),
        ],
        out_specs=whole(BLOCKS.shape),
        scratch_shapes=[
            pltpu.VMEM((BASIS, POINTS), jnp.bfloat16),
            pltpu.VMEM((SLOTS_ALL, ROWS, LANES), jnp.bfloat16),
        ],
        compiler_params=params(),
        cost_estimate=pl.CostEstimate(flops=2 * TASKS * BASIS * BASIS * POINTS, bytes_accessed=14 << 20, transcendentals=0),
        name="matrices",
    )(labels, phi, box_potential)

    def fast(results, held, density, margin, places, routes, inverse):
        return exchanged(inverse, routes, held, results, density, margin)

    def dense(results, held, density, margin, places, routes, inverse):
        outgoing = packed(places, density.reshape(PAIRS, BF, BF), SLOTS_ALL)
        arrived = by_plane(lax.all_to_all(outgoing.reshape(PEERS, 64, LANES), ALL, 0, 0, tiled=True))
        returned = lax.all_to_all(by_mesh(results.reshape(PEERS, 64, LANES)), ALL, 0, 0, tiled=True)
        back = returned.reshape(BLOCKS.shape)[places]
        wide = margin_of(density, margin).transpose(0, 2, 1, 3).reshape(atoms_here, BF, offsets * BF)
        return (
            arrived.reshape(BLOCKS.shape),
            jnp.pad(back, ((0, HELD - PAIRS), (0, 0), (0, 0))),
            jnp.pad(wide, ((0, 0), (0, 0), (0, BF))),
        )

    arrived, back, product = lax.cond(over, dense, fast, results, held, density, margin, places, routes, inverse)
    pickup = jnp.where(over, jnp.arange(PAIRS, dtype=jnp.int32), spots)

    grid_rows, ks_blocks, margin_product = pl.pallas_call(
        grid_kernel,
        out_shape=(
            jax.ShapeDtypeStruct((TASKS, 1, POINTS), jnp.float32),
            jax.ShapeDtypeStruct((PAIRS, BF, BF), jnp.bfloat16),
            jax.ShapeDtypeStruct((PAIRS, BF, BF), jnp.bfloat16),
        ),
        grid=(TASKS,),
        in_specs=[
            SMEM,
            SMEM,
            whole(BLOCKS.shape),
            pl.BlockSpec((1, BASIS, POINTS), lambda t: (t, 0, 0)),
            whole((HELD, ROWS, LANES)),
            pl.BlockSpec((3, BF, 384), lambda t: (t, 0, 0)),
        ],
        out_specs=(
            pl.BlockSpec((1, 1, POINTS), lambda t: (t, 0, 0)),
            pl.BlockSpec((15, BF, BF), lambda t: (t, 0, 0)),
            pl.BlockSpec((15, BF, BF), lambda t: (t, 0, 0)),
        ),
        scratch_shapes=[
            pltpu.VMEM((SLOTS_ALL + 1, ROWS, LANES), jnp.float32),
            pltpu.VMEM((BASIS, BASIS), jnp.bfloat16),
        ],
        compiler_params=params(),
        name="collocate",
    )(labels, pickup, arrived, phi, back, product)
    density_grid = grid_rows.reshape(32, 1, 256)
    return density_grid, ks_blocks.reshape(atoms_here, offsets, BF, BF), margin_product.reshape(atoms_here, offsets, BF, BF)


def solution(mesh):
    placed = (
        P(ALL, None, None, None),
        P(ALL, None, None, None),
        P("row", None, "col"),
        P(ALL, None, None, None),
        P(ALL, None, None),
        P(ALL, None),
        P(ALL, None, None),
    )
    return jax.shard_map(
        local,
        mesh=mesh,
        in_specs=placed,
        out_specs=(P(None, "row", "col"), P(ALL, None, None, None), P(ALL, None, None, None)),
        check_vma=False,
    )
```

```python
import functools

import jax
import jax.numpy as jnp
from jax import lax
from jax.experimental import pallas as pl
from jax.experimental.pallas import tpu as pltpu
from jax.sharding import PartitionSpec as P

HALF = 2
PAIRS = 120
PEERS = 256
SLOTS_ALL = 512
ROWS = 32
LANES = 128
BF = 64
TASKS = 8
BASIS = 512
POINTS = 1024
ALL = ("row", "col")
ZS = 8
PLANE = 32
CAP = 28
HELD = ZS * CAP
MESH = pl.DeviceIdType.MESH
VMEM_LIMIT = 56 * 1024 * 1024


def padded(array, sides, width):
    for axis, dim in sides:
        size, length = (lax.axis_size(axis), array.shape[dim])
        up = [(i, (i + 1) % size) for i in range(size)]
        down = [(j, i) for i, j in up]
        last = lax.slice_in_dim(array, length - width, length, axis=dim)
        first = lax.slice_in_dim(array, 0, width, axis=dim)
        before = lax.ppermute(last, axis, up)
        after = lax.ppermute(first, axis, down)
        array = jnp.concatenate([before, array, after], axis=dim)
    return array


def margin_of(density, margin):
    atoms_here = density.shape[0]
    offsets = density.shape[1]
    extended = padded(margin, ((ALL, 0),), HALF)
    columns = []
    for offset in range(offsets):
        lowest = max(0, offset - HALF)
        highest = min(offsets - 1, offset + HALF)
        left_blocks = density[:, lowest : highest + 1]
        right_blocks = jnp.stack(
            [extended[middle : middle + atoms_here, offset - middle + HALF] for middle in range(lowest, highest + 1)],
            axis=1,
        )
        columns.append(jnp.einsum("amik,amkj->aij", left_blocks, right_blocks, preferred_element_type=jnp.float32))
    return jnp.stack(columns, axis=1).astype(jnp.bfloat16)


def pack_kernel(place, density, out):
    def body(step, carry):
        for inner in range(8):
            pair = step * 8 + inner
            block = density[pair]
            spot = place[pair]
            out[spot, :, 0:BF] = block[0:ROWS]
            out[spot, :, BF:LANES] = block[ROWS:BF]
        return carry

    lax.fori_loop(0, PAIRS // 8, body, 0)


PSTEPS = [
    (dy, dx, dc)
    for dy, dx in (
        (2, 2), (1, 3), (3, 1), (1, 1), (3, 3), (2, 1), (2, 3), (1, 2), (3, 2), (0, 2), (2, 0), (0, 1), (0, 3), (1, 0), (3, 0), (0, 0),
    )
    for dc in (0, 1)
    if (dy, dx, dc) != (0, 0, 0)
]
ZSTEPS = (4, 3, 5, 2, 6, 1, 7)
WIDE = 640


def exchange_kernel(
    inverse, routes, picks, held, results, density, margin, arrived, back, product,
    table, chosen, zgot, pgot, zput, pput, dens, marg, even, odd, zs, zr, ps, pr, zs2, zr2, ps2, pr2, hs, hr, own,
):
    row, col = lax.axis_index("row"), lax.axis_index("col")
    y, x, high = row // 8, lax.rem(row // 2, 4), lax.rem(row, 2)
    low, core = col // 2, lax.rem(col, 2)
    z = high * 4 + low
    here = (y * 4 + x) * 2 + core
    flat = row * 8 + col
    after, before = lax.rem(flat + 1, PEERS), lax.rem(flat + PEERS - 1, PEERS)
    after, before = (after // 8, lax.rem(after, 8)), (before // 8, lax.rem(before, 8))

    def along(step):
        to = lax.rem(z + step, ZS)
        return to, (y * 8 + x * 2 + to // 4, lax.rem(to, 4) * 2 + core)

    def across(steps):
        dy, dx, dc = steps
        to_y, to_x, to_c = lax.rem(y + dy, 4), lax.rem(x + dx, 4), lax.rem(core + dc, 2)
        return (to_y * 4 + to_x) * 2 + to_c, (to_y * 8 + to_x * 2 + high, low * 2 + to_c)

    def send(source, target, sent, received, where):
        copy = pltpu.make_async_remote_copy(
            src_ref=source, dst_ref=target, send_sem=sent, recv_sem=received, device_id=where, device_id_type=MESH
        )
        copy.start()
        return copy

    def keep(source, target, semaphore):
        copy = pltpu.make_async_copy(source, target, semaphore)
        copy.start()
        return copy

    def rows(ref, start, count):
        return ref.at[pl.ds(start * count, count)]

    barrier = pltpu.get_barrier_semaphore()
    for step in ZSTEPS:
        pl.semaphore_signal(barrier, inc=1, device_id=along(step)[1], device_id_type=MESH)
    for steps in PSTEPS:
        pl.semaphore_signal(barrier, inc=1, device_id=across(steps)[1], device_id_type=MESH)
    for where in (after, before):
        pl.semaphore_signal(barrier, inc=1, device_id=where, device_id_type=MESH)
    filled = keep(results, table, own.at[6])
    loads = [keep(density, dens, own.at[0]), keep(margin, marg.at[pl.ds(2, 24)], own.at[1])]
    pl.semaphore_wait(barrier, len(ZSTEPS) + len(PSTEPS) + 2)

    halos = [
        send(margin.at[pl.ds(22, 2)], marg.at[pl.ds(0, 2)], hs.at[0], hr.at[0], after),
        send(margin.at[pl.ds(0, 2)], marg.at[pl.ds(26, 2)], hs.at[1], hr.at[1], before),
    ]
    first_z, first_p = [], []
    for number in range(len(ZSTEPS)):
        to, where = along(ZSTEPS[number])
        first_z.append(send(rows(held, to, CAP), rows(zgot, z, CAP), zs.at[number], zr.at[number], where))
    own_z = keep(rows(held, z, CAP), rows(zgot, z, CAP), own.at[2])
    filled.wait()

    def gather_source(to):
        def body(step, carry):
            for inner in range(8):
                spot = to * 16 + step * 8 + inner
                chosen[spot] = table[picks[spot]]
            return carry

        lax.fori_loop(0, 2, body, 0)

    def source(number):
        to, where = across(PSTEPS[number])
        return send(rows(chosen, to, 16), rows(pgot, here, 16), ps.at[number], pr.at[number], where)

    gather_source(across(PSTEPS[0])[0])
    for number in range(1, len(PSTEPS)):
        gather_source(across(PSTEPS[number])[0])
        first_p.append(source(number - 1))
    gather_source(here)
    first_p.append(source(len(PSTEPS) - 1))
    own_p = keep(rows(chosen, here, 16), rows(pgot, here, 16), own.at[3])

    def clear(atom, carry):
        even[atom] = jnp.zeros((BF, WIDE), jnp.bfloat16)
        odd[atom] = jnp.zeros((BF, WIDE), jnp.bfloat16)
        return carry

    lax.fori_loop(0, 28, clear, 0)
    for copy in loads + halos:
        copy.wait()

    def widen(atom, carry):
        for block in range(5):
            piece = marg[atom, block]
            even[atom, :, (block + 2) * BF : (block + 3) * BF] = piece
            odd[atom, :, (block + 1) * BF : (block + 2) * BF] = piece
        return carry

    lax.fori_loop(0, 28, widen, 0)

    def multiply(atom, carry):
        total = jnp.zeros((BF, 384), jnp.float32)
        for middle in range(5):
            wide = even if middle % 2 == 0 else odd
            start = (4 - middle) // 2 * LANES
            total = total + jnp.dot(
                dens[atom, middle], wide[atom + middle, :, start : start + 384], preferred_element_type=jnp.float32
            )
        product[atom] = total.astype(jnp.bfloat16)
        return carry

    lax.fori_loop(0, 24, multiply, 0)

    for copy in first_z:
        copy.wait()
    own_z.wait()

    def gather_owner(to):
        def body(step, carry):
            for inner in range(8):
                spot = to * 16 + step * 8 + inner
                pput[spot] = zgot[inverse[spot]]
            return carry

        lax.fori_loop(0, 2, body, 0)

    def owner(number):
        to, where = across(PSTEPS[number])
        return send(rows(pput, to, 16), rows(arrived, here, 16), ps2.at[number], pr2.at[number], where)

    second = []
    gather_owner(across(PSTEPS[0])[0])
    for number in range(1, len(PSTEPS)):
        gather_owner(across(PSTEPS[number])[0])
        second.append(owner(number - 1))
    gather_owner(here)
    second.append(owner(len(PSTEPS) - 1))

    for copy in first_p:
        copy.wait()
    own_p.wait()

    def gather_holder(to):
        def body(step, carry):
            for inner in range(4):
                spot = to * CAP + step * 4 + inner
                zput[spot] = pgot[routes[spot]]
            return carry

        lax.fori_loop(0, CAP // 4, body, 0)

    def holder(number):
        to, where = along(ZSTEPS[number])
        return send(rows(zput, to, CAP), rows(back, z, CAP), zs2.at[number], zr2.at[number], where)

    gather_holder(along(ZSTEPS[0])[0])
    for number in range(1, len(ZSTEPS)):
        gather_holder(along(ZSTEPS[number])[0])
        second.append(holder(number - 1))
    gather_holder(z)
    second.append(holder(len(ZSTEPS) - 1))
    second.append(keep(rows(pput, here, 16), rows(arrived, here, 16), own.at[4]))
    second.append(keep(rows(zput, z, CAP), rows(back, z, CAP), own.at[5]))
    for copy in second:
        copy.wait()


def exchanged(inverse, routes, picks, held, results, density, margin):
    hbm = pl.BlockSpec(memory_space=pl.ANY)
    dma = pltpu.SemaphoreType.DMA
    return pl.pallas_call(
        exchange_kernel,
        out_shape=(
            BLOCKS,
            jax.ShapeDtypeStruct((HELD, ROWS, LANES), jnp.bfloat16),
            jax.ShapeDtypeStruct((24, BF, 384), jnp.bfloat16),
        ),
        in_specs=[SMEM, SMEM, SMEM, hbm, hbm, hbm, hbm],
        out_specs=(hbm, hbm, VM),
        scratch_shapes=[
            pltpu.VMEM((SLOTS_ALL, ROWS, LANES), jnp.bfloat16),
            pltpu.VMEM((SLOTS_ALL, ROWS, LANES), jnp.bfloat16),
            pltpu.VMEM((HELD, ROWS, LANES), jnp.bfloat16),
            pltpu.VMEM((SLOTS_ALL, ROWS, LANES), jnp.bfloat16),
            pltpu.VMEM((HELD, ROWS, LANES), jnp.bfloat16),
            pltpu.VMEM((SLOTS_ALL, ROWS, LANES), jnp.bfloat16),
            pltpu.VMEM((24, 5, BF, BF), jnp.bfloat16),
            pltpu.VMEM((28, 5, BF, BF), jnp.bfloat16),
            pltpu.VMEM((28, BF, WIDE), jnp.bfloat16),
            pltpu.VMEM((28, BF, WIDE), jnp.bfloat16),
            dma((7,)), dma((7,)), dma((31,)), dma((31,)),
            dma((7,)), dma((7,)), dma((31,)), dma((31,)),
            dma((2,)), dma((2,)), dma((7,)),
        ],
        compiler_params=params(collective_id=0, has_side_effects=True),
        name="exchange",
    )(inverse, routes, picks, held, results, density, margin)


def notice_kernel(
    which, table, potential, density, got, pencil, held, zgot, other, zs, zr, ps, pr, qs, qr, us, ur, own
):
    row, col = lax.axis_index("row"), lax.axis_index("col")
    y, x, high = row // 8, lax.rem(row // 2, 4), lax.rem(row, 2)
    low, core = col // 2, lax.rem(col, 2)
    z = high * 4 + low
    here = (y * 4 + x) * 2 + core
    flipped = y * 8 + x * 2 + (1 - high)

    def along(step):
        to = lax.rem(z + step, ZS)
        return to, (y * 8 + x * 2 + to // 4, lax.rem(to, 4) * 2 + core)

    def across(steps):
        dy, dx, dc = steps
        to_y, to_x, to_c = lax.rem(y + dy, 4), lax.rem(x + dx, 4), lax.rem(core + dc, 2)
        return (to_y * 4 + to_x) * 2 + to_c, (to_y * 8 + to_x * 2 + high, low * 2 + to_c)

    def send(source, target, sent, received, where):
        copy = pltpu.make_async_remote_copy(
            src_ref=source, dst_ref=target, send_sem=sent, recv_sem=received, device_id=where, device_id_type=MESH
        )
        copy.start()
        return copy

    def keep(source, target, semaphore):
        copy = pltpu.make_async_copy(source, target, semaphore)
        copy.start()
        return copy

    barrier = pltpu.get_barrier_semaphore()
    for step in ZSTEPS:
        pl.semaphore_signal(barrier, inc=1, device_id=along(step)[1], device_id_type=MESH)
    for steps in PSTEPS:
        pl.semaphore_signal(barrier, inc=1, device_id=across(steps)[1], device_id_type=MESH)
    pl.semaphore_wait(barrier, len(ZSTEPS) + len(PSTEPS))

    first = [send(potential, other, zs.at[7], zr.at[7], along(4)[1])]
    for number in range(len(ZSTEPS)):
        to, where = along(ZSTEPS[number])
        first.append(send(table.at[to], zgot.at[z], zs.at[number], zr.at[number], where))
    first.append(keep(table.at[z], zgot.at[z], own.at[0]))

    def pack(step, carry):
        for inner in range(8):
            spot = step * 8 + inner
            block = density[which[spot]]
            held[spot, :, 0:BF] = block[0:ROWS]
            held[spot, :, BF:LANES] = block[ROWS:BF]
        return carry

    lax.fori_loop(0, HELD // 8, pack, 0)
    for copy in first:
        copy.wait()

    second, line = [], 0
    for number in range(len(PSTEPS)):
        to, where = across(PSTEPS[number])
        second.append(send(zgot.at[:, to], got.at[here], ps.at[number], pr.at[number], where))
        if PSTEPS[number][2] == 0:
            second.append(send(potential.at[where[0]], pencil.at[row], qs.at[line], qr.at[line], where))
            second.append(send(other.at[where[0]], pencil.at[flipped], us.at[line], ur.at[line], where))
            line += 1
    second.append(keep(zgot.at[:, here], got.at[here], own.at[1]))
    second.append(keep(potential.at[row], pencil.at[row], own.at[2]))
    second.append(keep(other.at[row], pencil.at[flipped], own.at[3]))
    for copy in second:
        copy.wait()


def noticed(which, table, potential, flat):
    dma = pltpu.SemaphoreType.DMA
    return pl.pallas_call(
        notice_kernel,
        out_shape=(
            jax.ShapeDtypeStruct((PLANE, ZS, 1, LANES), jnp.int32),
            jax.ShapeDtypeStruct((32, 1, 256), jnp.float32),
            jax.ShapeDtypeStruct((HELD, ROWS, LANES), jnp.bfloat16),
        ),
        in_specs=[SMEM, VM, VM, VM],
        out_specs=(VM, VM, VM),
        scratch_shapes=[
            pltpu.VMEM((ZS, PLANE, 1, LANES), jnp.int32),
            pltpu.VMEM((32, 1, 256), jnp.float32),
            dma((8,)), dma((8,)), dma((31,)), dma((31,)), dma((15,)), dma((15,)), dma((15,)), dma((15,)), dma((4,)),
        ],
        compiler_params=params(collective_id=1, has_side_effects=True),
        name="notices",
    )(which, table, potential, flat)


def matrix_kernel(basis, potential, table, scaled):
    phi = basis[0]
    scaled[...] = (phi.astype(jnp.float32) * potential[0]).astype(jnp.bfloat16)
    full = lax.dot_general(
        scaled[...], phi, (((1,), (1,)), ((), ())), preferred_element_type=jnp.float32
    )
    left = lax.broadcasted_iota(jnp.int32, (ROWS, LANES), 1) < BF
    for first in range(8):
        for pair in range(4):
            columns = slice(pair * LANES, (pair + 1) * LANES)
            top = full[first * BF : first * BF + ROWS, columns]
            low = full[first * BF + ROWS : (first + 1) * BF, columns]
            spot = first * 8 + 2 * pair
            table[spot] = jnp.where(left, top, pltpu.roll(low, BF, 1)).astype(jnp.bfloat16)
            table[spot + 1] = jnp.where(left, pltpu.roll(top, BF, 1), low).astype(jnp.bfloat16)


def grid_kernel(label, place, blocks, basis, back, product, out, ks, margins, table, weights):
    task = pl.program_id(0)

    @pl.when(task == 0)
    def _():
        def clear(step, carry):
            for inner in range(8):
                table[step * 8 + inner] = jnp.zeros((ROWS, LANES), jnp.float32)
            return carry

        lax.fori_loop(0, SLOTS_ALL // 8, clear, 0)

        def body(step, carry):
            for inner in range(8):
                slot = step * 8 + inner
                which = label[slot]
                spot = jnp.where(which < 0, SLOTS_ALL, which)
                table[spot] = table[spot] + blocks[slot].astype(jnp.float32)
            return carry

        lax.fori_loop(0, SLOTS_ALL // 8, body, 0)

    left = lax.broadcasted_iota(jnp.int32, (ROWS, LANES), 1) < BF
    for first in range(8):
        for pair in range(4):
            spot = task * 64 + first * 8 + 2 * pair
            one = table[spot]
            two = table[spot + 1]
            columns = slice(pair * LANES, (pair + 1) * LANES)
            weights[first * BF : first * BF + ROWS, columns] = jnp.where(left, one, pltpu.roll(two, BF, 1)).astype(
                jnp.bfloat16
            )
            weights[first * BF + ROWS : (first + 1) * BF, columns] = jnp.where(left, pltpu.roll(one, BF, 1), two).astype(
                jnp.bfloat16
            )
    for piece in range(4):
        columns = slice(piece * 256, (piece + 1) * 256)
        phi = basis[0, :, columns]
        weighted = jnp.dot(weights[...], phi, preferred_element_type=jnp.float32)
        out[0, :, columns] = jnp.sum(phi.astype(jnp.float32) * weighted, axis=0, keepdims=True)
    for pair in range(15):
        block = back[place[task * 15 + pair]]
        ks[pair, 0:ROWS] = block[:, 0:BF]
        ks[pair, ROWS:BF] = block[:, BF:LANES]
    for atom in range(3):
        for offset in range(5):
            margins[atom * 5 + offset] = product[atom, :, offset * BF : (offset + 1) * BF]


def params(**more):
    return pltpu.CompilerParams(vmem_limit_bytes=VMEM_LIMIT, **more)


SMEM = pl.BlockSpec(memory_space=pltpu.SMEM)
VM = pl.BlockSpec(memory_space=pltpu.VMEM)
BLOCKS = jax.ShapeDtypeStruct((SLOTS_ALL, ROWS, LANES), jnp.bfloat16)


def whole(shape):
    return pl.BlockSpec(shape, lambda *_: (0,) * len(shape))


def packed(places, flat, blocks):
    return pl.pallas_call(
        pack_kernel,
        out_shape=jax.ShapeDtypeStruct((blocks, ROWS, LANES), jnp.bfloat16),
        in_specs=[SMEM, VM],
        out_specs=VM,
        compiler_params=params(),
        cost_estimate=pl.CostEstimate(flops=0, bytes_accessed=6 << 20, transcendentals=0),
        name="pack",
    )(places, flat)


def by_plane(values):
    rest = values.shape[1:]
    return values.reshape((16, 8, 2) + rest).swapaxes(1, 2).reshape((PEERS,) + rest)


def by_mesh(values):
    rest = values.shape[1:]
    return values.reshape((16, 2, 8) + rest).swapaxes(1, 2).reshape((PEERS,) + rest)


def local(density, margin, potential, basis_values, pair_owner, pair_box, pair_slots):
    atoms_here, offsets = density.shape[:2]
    row, col = lax.axis_index("row"), lax.axis_index("col")
    owners = pair_owner.reshape(PAIRS)
    planes = (owners // 8) % 2 * 4 + owners % 8 // 2
    inside = owners // 16 * 2 + owners % 2
    order = jnp.arange(PAIRS, dtype=jnp.int32)
    before = order[:, None] > order[None, :]
    ranks = jnp.sum(((owners[:, None] == owners[None, :]) & before).astype(jnp.int32), axis=1)
    turns = jnp.sum(((planes[:, None] == planes[None, :]) & before).astype(jnp.int32), axis=1)
    places = owners * 2 + ranks
    spots = jnp.where(turns < CAP, planes * CAP + turns, HELD)
    flat = density.reshape(PAIRS, BF, BF)
    which = jnp.sum(
        jnp.where(jnp.arange(HELD, dtype=jnp.int32)[:, None] == spots[None, :], order[None, :], 0), axis=1
    )
    over = jnp.max(turns) >= CAP
    lanes = jnp.arange(LANES, dtype=jnp.int32)[None, :]
    peers = jnp.arange(PEERS, dtype=jnp.int32)[:, None]

    def column(values):
        return values.reshape(PAIRS, 1)

    box, one, two = column(pair_box), column(pair_slots[..., 0]), column(pair_slots[..., 1])
    field = jnp.where(lanes < 2, box, jnp.where(lanes < 4, one, two)) + 1
    to_owner = jnp.where((lanes < 6) & (lanes % 2 == column(ranks)), field, 0)
    to_plane = jnp.where(lanes - 8 == column(turns), column(inside * 2 + ranks) + 1, 0)
    at_owner = peers == (planes * PLANE + inside)[None, :]
    at_plane = peers // PLANE == planes[None, :]

    def listed(chosen, values):
        return jnp.dot(chosen.astype(jnp.bfloat16), values.astype(jnp.bfloat16), preferred_element_type=jnp.float32)

    table = (listed(at_owner, to_owner) + listed(at_plane, to_plane)).astype(jnp.int32) - 1
    table = jnp.where(lanes == 6, over.astype(jnp.int32), table)
    got, pencil, held = noticed(
        which, table.reshape(ZS, PLANE, 1, LANES), potential.reshape(32, 1, 256), flat
    )
    box_potential = pencil.reshape(TASKS, 1, POINTS)
    got = got.reshape(PEERS, LANES)
    over = jnp.max(got[:, 6]) > 0
    tags = got[:, 0:2] * 64 + got[:, 2:4] * 8 + got[:, 4:6]
    labels = jnp.where(got[:, 0:2] < 0, -1, tags).reshape(SLOTS_ALL)
    here = row // 2 * 2 + col % 2
    targets = lax.dynamic_slice(got, (here * ZS, 8), (ZS, CAP))
    number = jnp.arange(HELD, dtype=jnp.int32)
    targets = targets.reshape(HELD)
    routes = targets // 2 * 16 + number // CAP * 2 + targets % 2
    inverse = jnp.sum(
        jnp.where(
            (jnp.arange(SLOTS_ALL, dtype=jnp.int32)[:, None] == routes[None, :]) & (targets >= 0)[None, :], number[None, :], 0
        ),
        axis=1,
    )
    routes = jnp.where(targets < 0, 0, routes)

    phi = basis_values.reshape(TASKS, BASIS, POINTS)
    results = pl.pallas_call(
        matrix_kernel,
        out_shape=BLOCKS,
        grid=(TASKS,),
        in_specs=[
            pl.BlockSpec((1, BASIS, POINTS), lambda t: (t, 0, 0)),
            pl.BlockSpec((1, 1, POINTS), lambda t: (t, 0, 0)),
        ],
        out_specs=pl.BlockSpec((64, ROWS, LANES), lambda t: (t, 0, 0)),
        scratch_shapes=[pltpu.VMEM((BASIS, POINTS), jnp.bfloat16)],
        compiler_params=params(),
        cost_estimate=pl.CostEstimate(flops=2 * TASKS * BASIS * BASIS * POINTS, bytes_accessed=14 << 20, transcendentals=0),
        name="matrices",
    )(phi, box_potential)
    picks = jnp.maximum(labels, 0)

    def fast(results, held, density, margin, places, routes, inverse, picks):
        return exchanged(inverse, routes, picks, held, results, density, margin)

    def dense(results, held, density, margin, places, routes, inverse, picks):
        results = results[picks]
        outgoing = packed(places, density.reshape(PAIRS, BF, BF), SLOTS_ALL)
        arrived = by_plane(lax.all_to_all(outgoing.reshape(PEERS, 64, LANES), ALL, 0, 0, tiled=True))
        returned = lax.all_to_all(by_mesh(results.reshape(PEERS, 64, LANES)), ALL, 0, 0, tiled=True)
        back = returned.reshape(BLOCKS.shape)[places]
        wide = margin_of(density, margin).transpose(0, 2, 1, 3).reshape(atoms_here, BF, offsets * BF)
        return (
            arrived.reshape(BLOCKS.shape),
            jnp.pad(back, ((0, HELD - PAIRS), (0, 0), (0, 0))),
            jnp.pad(wide, ((0, 0), (0, 0), (0, BF))),
        )

    arrived, back, product = lax.cond(over, dense, fast, results, held, density, margin, places, routes, inverse, picks)
    pickup = jnp.where(over, jnp.arange(PAIRS, dtype=jnp.int32), spots)

    grid_rows, ks_blocks, margin_product = pl.pallas_call(
        grid_kernel,
        out_shape=(
            jax.ShapeDtypeStruct((TASKS, 1, POINTS), jnp.float32),
            jax.ShapeDtypeStruct((PAIRS, BF, BF), jnp.bfloat16),
            jax.ShapeDtypeStruct((PAIRS, BF, BF), jnp.bfloat16),
        ),
        grid=(TASKS,),
        in_specs=[
            SMEM,
            SMEM,
            whole(BLOCKS.shape),
            pl.BlockSpec((1, BASIS, POINTS), lambda t: (t, 0, 0)),
            whole((HELD, ROWS, LANES)),
            pl.BlockSpec((3, BF, 384), lambda t: (t, 0, 0)),
        ],
        out_specs=(
            pl.BlockSpec((1, 1, POINTS), lambda t: (t, 0, 0)),
            pl.BlockSpec((15, BF, BF), lambda t: (t, 0, 0)),
            pl.BlockSpec((15, BF, BF), lambda t: (t, 0, 0)),
        ),
        scratch_shapes=[
            pltpu.VMEM((SLOTS_ALL + 1, ROWS, LANES), jnp.float32),
            pltpu.VMEM((BASIS, BASIS), jnp.bfloat16),
        ],
        compiler_params=params(),
        name="collocate",
    )(labels, pickup, arrived, phi, back, product)
    density_grid = grid_rows.reshape(32, 1, 256)
    return density_grid, ks_blocks.reshape(atoms_here, offsets, BF, BF), margin_product.reshape(atoms_here, offsets, BF, BF)


def solution(mesh):
    placed = (
        P(ALL, None, None, None),
        P(ALL, None, None, None),
        P("row", None, "col"),
        P(ALL, None, None, None),
        P(ALL, None, None),
        P(ALL, None),
        P(ALL, None, None),
    )
    return jax.shard_map(
        local,
        mesh=mesh,
        in_specs=placed,
        out_specs=(P(None, "row", "col"), P(ALL, None, None, None), P(ALL, None, None, None)),
        check_vma=False,
    )
```
